32 devices in a mesh: dp: 8 (over z, y), tp: 4 (over x, core).
Axes of the slice: x: 2, y: 2, z: 4, core: 2. Of those that a mesh axis runs over, the one named last changes fastest.
Arguments:
- frames: bfloat16 [24, 1024, 512], P('dp', 'tp'), may hold values from -6 to 6
- cotangent: bfloat16 [24, 1024, 512], P('dp', 'tp'), may hold values from -6 to 6
- lengths: int32 [24], P('dp'), may hold values from 64 to 1024, as said below
- conv_weight: float32 [512, 7], P(('dp', 'tp')), may hold values from -2 to 2
- conv_bias: float32 [512], P(('dp', 'tp')), may hold values from -0.6 to 0.6
- norm_gain: float32 [512], P(('dp', 'tp')), may hold values from 0.5 to 1.5
- norm_bias: float32 [512], P(('dp', 'tp')), may hold values from -0.6 to 0.6
- up_weight: float32 [512, 1536], P('dp', 'tp'), may hold values from -0.25 to 0.25
- up_bias: float32 [1536], P(('dp', 'tp')), may hold values from -0.6 to 0.6
- down_weight: float32 [512, 1536], P('dp', 'tp'), may hold values from -0.15625 to 0.15625
- down_bias: float32 [512], P(('dp', 'tp')), may hold values from -0.6 to 0.6
- layer_scale: float32 [512], P(('dp', 'tp')), may hold values from 0.25 to 1.75
- moment_conv_weight: float32 [512, 7], P(('dp', 'tp')), may hold values from -36 to 36
- moment_conv_bias: float32 [512], P(('dp', 'tp')), may hold values from -36 to 36
- moment_norm_gain: float32 [512], P(('dp', 'tp')), may hold values from -36 to 36
- moment_norm_bias: float32 [512], P(('dp', 'tp')), may hold values from -36 to 36
- moment_up_weight: float32 [512, 1536], P('dp', 'tp'), may hold values from -36 to 36
- moment_up_bias: float32 [1536], P(('dp', 'tp')), may hold values from -36 to 36
- moment_down_weight: float32 [512, 1536], P('dp', 'tp'), may hold values from -36 to 36
- moment_down_bias: float32 [512], P(('dp', 'tp')), may hold values from -36 to 36
- moment_layer_scale: float32 [512], P(('dp', 'tp')), may hold values from -36 to 36
- square_conv_weight: float32 [512, 7], P(('dp', 'tp')), may hold values from 1 to 9
- square_conv_bias: float32 [512], P(('dp', 'tp')), may hold values from 1 to 9
- square_norm_gain: float32 [512], P(('dp', 'tp')), may hold values from 1 to 9
- square_norm_bias: float32 [512], P(('dp', 'tp')), may hold values from 1 to 9
- square_up_weight: float32 [512, 1536], P('dp', 'tp'), may hold values from 1 to 9
- square_up_bias: float32 [1536], P(('dp', 'tp')), may hold values from 1 to 9
- square_down_weight: float32 [512, 1536], P('dp', 'tp'), may hold values from 1 to 9
- square_down_bias: float32 [512], P(('dp', 'tp')), may hold values from 1 to 9
- square_layer_scale: float32 [512], P(('dp', 'tp')), may hold values from 1 to 9
Outputs:
- output: float32 [24, 1024, 512], P('dp', 'tp')
- input_grad: float32 [24, 1024, 512], P('dp', 'tp')
- grad_conv_weight: float32 [512, 7], P(('dp', 'tp'))
- next_conv_weight: float32 [512, 7], P(('dp', 'tp'))
- next_moment_conv_weight: float32 [512, 7], P(('dp', 'tp'))
- next_square_conv_weight: float32 [512, 7], P(('dp', 'tp'))
- grad_conv_bias: float32 [512], P(('dp', 'tp'))
- next_conv_bias: float32 [512], P(('dp', 'tp'))
- next_moment_conv_bias: float32 [512], P(('dp', 'tp'))
- next_square_conv_bias: float32 [512], P(('dp', 'tp'))
- grad_norm_gain: float32 [512], P(('dp', 'tp'))
- update_norm_gain: float32 [512], P(('dp', 'tp'))
- next_moment_norm_gain: float32 [512], P(('dp', 'tp'))
- next_square_norm_gain: float32 [512], P(('dp', 'tp'))
- grad_norm_bias: float32 [512], P(('dp', 'tp'))
- next_norm_bias: float32 [512], P(('dp', 'tp'))
- next_moment_norm_bias: float32 [512], P(('dp', 'tp'))
- next_square_norm_bias: float32 [512], P(('dp', 'tp'))
- grad_up_weight: float32 [512, 1536], P('dp', 'tp')
- next_up_weight: float32 [512, 1536], P('dp', 'tp')
- next_moment_up_weight: float32 [512, 1536], P('dp', 'tp')
- next_square_up_weight: float32 [512, 1536], P('dp', 'tp')
- grad_up_bias: float32 [1536], P(('dp', 'tp'))
- next_up_bias: float32 [1536], P(('dp', 'tp'))
- next_moment_up_bias: float32 [1536], P(('dp', 'tp'))
- next_square_up_bias: float32 [1536], P(('dp', 'tp'))
- grad_down_weight: float32 [512, 1536], P('dp', 'tp')
- next_down_weight: float32 [512, 1536], P('dp', 'tp')
- next_moment_down_weight: float32 [512, 1536], P('dp', 'tp')
- next_square_down_weight: float32 [512, 1536], P('dp', 'tp')
- grad_down_bias: float32 [512], P(('dp', 'tp'))
- next_down_bias: float32 [512], P(('dp', 'tp'))
- next_moment_down_bias: float32 [512], P(('dp', 'tp'))
- next_square_down_bias: float32 [512], P(('dp', 'tp'))
- grad_layer_scale: float32 [512], P(('dp', 'tp'))
- update_layer_scale: float32 [512], P(('dp', 'tp'))
- next_moment_layer_scale: float32 [512], P(('dp', 'tp'))
- next_square_layer_scale: float32 [512], P(('dp', 'tp'))
The draws below stay inside these ranges and needn't reach their ends.
Inputs may be any that keep to these rules, and one draw needn't show every extreme that they name: `lengths`: each slot's true frame count lies between 64 and 1024; in every draw at least one slot holds 1024 true frames.
All inputs are finite; a program needn't handle non-finite values.
Results may differ from the reference program's by a relative error of at most 0.0079.
Values may be sent and summed in bfloat16 or wider, within the bound.
No kernel may reach another device: no remote copies, remote signals or barrier semaphores. Data moves between devices by JAX's collectives and lax.ppermute only.
A program may use at most 128 MiB of HBM per device.

```python
import math
import jax
import jax.numpy as jnp
from jax import lax

C = 512
H = 1536
KERNEL = 7
STEP = 4
SLOT_LEN = 1024
MIN_LEN = 64
SLOTS = 24


def draw_lengths(key, part):
    first_key, second_key = jax.random.split(jax.random.fold_in(key, 11))
    drawn_lengths = jax.random.randint(first_key, (SLOTS,), MIN_LEN, SLOT_LEN + 1, dtype=jnp.int32)
    chosen_slot = jax.random.randint(second_key, (), 0, SLOTS, dtype=jnp.int32)
    slot_ids = jnp.arange(SLOTS, dtype=jnp.int32)
    return jnp.where(slot_ids == chosen_slot, jnp.int32(SLOT_LEN), drawn_lengths).astype(jnp.int32)


def block_levels(own_key, dims, cuts, least, top_value):
    def one(position, parts):
        draws = jax.random.uniform(jax.random.fold_in(jax.random.fold_in(own_key, 6), position), (parts,), jnp.float32, least / len(cuts), top_value / len(cuts))
        return jnp.repeat(jnp.exp(draws), dims[position] // parts).reshape((-1,) + (1,) * (len(dims) - position - 1))

    factor_of = one(*cuts[0])
    for cut in cuts[1:]:
        factor_of = factor_of * one(*cut)
    return factor_of


def noise(key, extent, scale, bound, shards=(), kind=jnp.bfloat16):
    values = jax.random.normal(key, extent, jnp.float32) * scale
    if len(shards) > 0:
        values = block_levels(key, extent, shards, -0.22, 0.18) * values
    return jnp.clip(values, min=-bound, max=bound).astype(kind)


def setup_inputs(seed: int = 0) -> dict:
    key_list = jax.random.split(jax.random.key(seed), 31)
    return {
        "frames": noise(key_list[0], (SLOTS, SLOT_LEN, C), 1.0, 6.0, ((0, 8), (1, 4))),
        "cotangent": noise(key_list[1], (SLOTS, SLOT_LEN, C), 1.0, 6.0, ((0, 8), (1, 4))),
        "lengths": draw_lengths(jax.random.fold_in(key_list[30], 71), 0),
        "conv_weight": noise(key_list[3], (C, KERNEL), KERNEL ** -0.5, 2.0, ((0, 32),), jnp.float32),
        "conv_bias": noise(key_list[4], (C,), 0.1, 0.6, ((0, 32),), jnp.float32),
        "norm_gain": jnp.clip(1.0 + 0.1 * jax.random.normal(key_list[5], (C,), jnp.float32), 0.5, 1.5),
        "norm_bias": noise(key_list[6], (C,), 0.1, 0.6, ((0, 32),), jnp.float32),
        "up_weight": noise(key_list[7], (C, H), C ** -0.5, 0.25, ((0, 8), (1, 4)), jnp.float32),
        "up_bias": noise(key_list[8], (H,), 0.1, 0.6, ((0, 32),), jnp.float32),
        "down_weight": noise(key_list[9], (C, H), H ** -0.5, 0.15625, ((0, 8), (1, 4)), jnp.float32),
        "down_bias": noise(key_list[10], (C,), 0.1, 0.6, ((0, 32),), jnp.float32),
        "layer_scale": jnp.clip(1.0 + 0.15 * jax.random.normal(key_list[11], (C,), jnp.float32), 0.25, 1.75),
        "moment_conv_weight": noise(key_list[12], (C, KERNEL), 6.0, 36.0, ((0, 32),), jnp.float32),
        "moment_conv_bias": noise(key_list[13], (C,), 6.0, 36.0, ((0, 32),), jnp.float32),
        "moment_norm_gain": noise(key_list[14], (C,), 6.0, 36.0, ((0, 32),), jnp.float32),
        "moment_norm_bias": noise(key_list[15], (C,), 6.0, 36.0, ((0, 32),), jnp.float32),
        "moment_up_weight": noise(key_list[16], (C, H), 6.0, 36.0, ((0, 8), (1, 4)), jnp.float32),
        "moment_up_bias": noise(key_list[17], (H,), 6.0, 36.0, ((0, 32),), jnp.float32),
        "moment_down_weight": noise(key_list[18], (C, H), 6.0, 36.0, ((0, 8), (1, 4)), jnp.float32),
        "moment_down_bias": noise(key_list[19], (C,), 6.0, 36.0, ((0, 32),), jnp.float32),
        "moment_layer_scale": noise(key_list[20], (C,), 6.0, 36.0, ((0, 32),), jnp.float32),
        "square_conv_weight": jnp.clip(jnp.exp(math.log(9.0) - 2.1972246 * jax.random.uniform(key_list[21], (C, KERNEL), jnp.float32) ** block_levels(key_list[21], (C, KERNEL), ((0, 32),), -0.2, 0.2)), 1.0, 9.0),
        "square_conv_bias": jnp.clip(jnp.exp(math.log(9.0) - 2.1972246 * jax.random.uniform(key_list[22], (C,), jnp.float32) ** block_levels(key_list[22], (C,), ((0, 32),), -0.2, 0.2)), 1.0, 9.0),
        "square_norm_gain": jnp.clip(jnp.exp(math.log(9.0) - 2.1972246 * jax.random.uniform(key_list[23], (C,), jnp.float32) ** block_levels(key_list[23], (C,), ((0, 32),), -0.2, 0.2)), 1.0, 9.0),
        "square_norm_bias": jnp.clip(jnp.exp(math.log(9.0) - 2.1972246 * jax.random.uniform(key_list[24], (C,), jnp.float32) ** block_levels(key_list[24], (C,), ((0, 32),), -0.2, 0.2)), 1.0, 9.0),
        "square_up_weight": jnp.clip(jnp.exp(math.log(9.0) - 2.1972246 * jax.random.uniform(key_list[25], (C, H), jnp.float32) ** block_levels(key_list[25], (C, H), ((0, 8), (1, 4)), -0.2, 0.2)), 1.0, 9.0),
        "square_up_bias": jnp.clip(jnp.exp(math.log(9.0) - 2.1972246 * jax.random.uniform(key_list[26], (H,), jnp.float32) ** block_levels(key_list[26], (H,), ((0, 32),), -0.2, 0.2)), 1.0, 9.0),
        "square_down_weight": jnp.clip(jnp.exp(math.log(9.0) - 2.1972246 * jax.random.uniform(key_list[27], (C, H), jnp.float32) ** block_levels(key_list[27], (C, H), ((0, 8), (1, 4)), -0.2, 0.2)), 1.0, 9.0),
        "square_down_bias": jnp.clip(jnp.exp(math.log(9.0) - 2.1972246 * jax.random.uniform(key_list[28], (C,), jnp.float32) ** block_levels(key_list[28], (C,), ((0, 32),), -0.2, 0.2)), 1.0, 9.0),
        "square_layer_scale": jnp.clip(jnp.exp(math.log(9.0) - 2.1972246 * jax.random.uniform(key_list[29], (C,), jnp.float32) ** block_levels(key_list[29], (C,), ((0, 32),), -0.2, 0.2)), 1.0, 9.0),
    }


@jax.custom_vjp
def low(v):
    return lax.optimization_barrier(v.astype(jnp.bfloat16)).astype(jnp.float32)

@jax.custom_vjp
def low_back(v):
    return v

def low_keep(v):
    return (low(v), None)

def low_pass(kept, grad):
    return (grad,)

def back_keep(v):
    return (v, None)

def back_low(kept, grad):
    return (low(grad),)
low.defvjp(low_keep, low_pass)
low_back.defvjp(back_keep, back_low)
norm_eps = 1e-06
learn_rate = 0.05
first_decay = 0.9
second_decay = 0.999
adam_eps = 1e-08
weight_decay = 0.1
update_flags = (False, False, True, False, False, False, False, False, True)

def conv_apply(padded, tap_weights, conv_shift, frames_out):
    result = conv_shift + padded[:, 0:frames_out, :] * tap_weights[:, 0]
    for offset in range(1, tap_weights.shape[1]):
        result = result + padded[:, offset:offset + frames_out, :] * tap_weights[:, offset]
    return result

def block_forward(frames_in, frame_mask, conv_weight, conv_bias, norm_gain, norm_bias, up_weight, up_bias, down_weight, down_bias, layer_scale):
    kernel_half = conv_weight.shape[1] // 2
    shifted = frames_in * frame_mask
    padded = jnp.pad(shifted, ((0, 0), (kernel_half, kernel_half), (0, 0)))
    conv_out = conv_apply(padded, conv_weight, conv_bias, frames_in.shape[1])
    centred = conv_out - lax.optimization_barrier(jnp.mean(conv_out, axis=-1, keepdims=True))
    inverse = lax.rsqrt(lax.optimization_barrier(jnp.mean(centred * centred, axis=-1, keepdims=True)) + norm_eps)
    normed = low(centred * inverse * norm_gain + norm_bias)
    hidden = low_back(jnp.einsum('slc,ch->slh', normed, low(up_weight), precision=lax.Precision.HIGHEST) + up_bias)
    active = low(jax.nn.gelu(hidden, approximate=False))
    branch = low_back(jnp.einsum('slh,ch->slc', active, low(down_weight), precision=lax.Precision.HIGHEST) + down_bias)
    return (frames_in + layer_scale * branch) * frame_mask

def adam_step(weights_now, gradient, moment, square, step_number):
    next_moment = first_decay * moment + (1.0 - first_decay) * gradient
    next_square = second_decay * square + (1.0 - second_decay) * gradient * gradient
    first_fix = 1.0 - jnp.power(jnp.float32(first_decay), step_number)
    second_fix = 1.0 - jnp.power(jnp.float32(second_decay), step_number)
    step_ratio = next_moment / first_fix / (jnp.sqrt(next_square / second_fix) + adam_eps)
    update = -(learn_rate * (step_ratio + weight_decay * weights_now))
    return (weights_now + update, next_moment, next_square, update)

def reference(frames, cotangent, lengths, conv_weight, conv_bias, norm_gain, norm_bias, up_weight, up_bias, down_weight, down_bias, layer_scale, moment_conv_weight, moment_conv_bias, moment_norm_gain, moment_norm_bias, moment_up_weight, moment_up_bias, moment_down_weight, moment_down_bias, moment_layer_scale, square_conv_weight, square_conv_bias, square_norm_gain, square_norm_bias, square_up_weight, square_up_bias, square_down_weight, square_down_bias, square_layer_scale):
    params = (conv_weight, conv_bias, norm_gain, norm_bias, up_weight, up_bias, down_weight, down_bias, layer_scale)
    moments = (moment_conv_weight, moment_conv_bias, moment_norm_gain, moment_norm_bias, moment_up_weight, moment_up_bias, moment_down_weight, moment_down_bias, moment_layer_scale)
    squares = (square_conv_weight, square_conv_bias, square_norm_gain, square_norm_bias, square_up_weight, square_up_bias, square_down_weight, square_down_bias, square_layer_scale)
    group_size = math.gcd(SLOTS, 4)
    block_count = SLOTS // group_size
    frame_blocks = frames.astype(jnp.float32).reshape(block_count, group_size, SLOT_LEN, C)
    cot_blocks = cotangent.astype(jnp.float32).reshape(block_count, group_size, SLOT_LEN, C)
    length_blocks = lengths.astype(jnp.int32).reshape(block_count, group_size)

    def one_block(grad_total, slot_block):
        frames_in, cot_in, length_in = slot_block
        positions = lax.broadcasted_iota(jnp.int32, (group_size, SLOT_LEN), 1)
        frame_mask = (positions < length_in[:, None]).astype(jnp.float32)[:, :, None]

        def forward(frames_arg, *param_args):
            return block_forward(frames_arg, frame_mask, *param_args)
        output_block, pull = jax.vjp(forward, frames_in, *params)
        pulled = pull(cot_in)
        grad_total = tuple((left + right for left, right in zip(grad_total, pulled[1:])))
        return (grad_total, (output_block, pulled[0]))
    start_total = tuple((jnp.zeros_like(weights_now) for weights_now in params))
    grad_total, (output_blocks, input_blocks) = lax.scan(one_block, start_total, (frame_blocks, cot_blocks, length_blocks))
    step_number = jnp.float32(STEP)
    flat = [output_blocks.reshape(SLOTS, SLOT_LEN, C), input_blocks.reshape(SLOTS, SLOT_LEN, C)]
    for weights_now, gradient, moment, square, use_update in zip(params, grad_total, moments, squares, update_flags):
        next_weights, next_moment, next_square, update = adam_step(weights_now, gradient, moment, square, step_number)
        shown = update if use_update else next_weights
        flat = flat + [gradient, shown, next_moment, next_square]
    return (flat[0], flat[1], flat[2], flat[3], flat[4], flat[5], flat[6], flat[7], flat[8], flat[9], flat[10], flat[11], flat[12], flat[13], flat[14], flat[15], flat[16], flat[17], flat[18], flat[19], flat[20], flat[21], flat[22], flat[23], flat[24], flat[25], flat[26], flat[27], flat[28], flat[29], flat[30], flat[31], flat[32], flat[33], flat[34], flat[35], flat[36], flat[37])
```

```python
import functools

import jax
import jax.numpy as jnp
from jax import lax
from jax.experimental import pallas as pl
from jax.experimental.pallas import tpu as pltpu
from jax.sharding import PartitionSpec as P

STEP = 4


norm_eps = 1e-06
learn_rate = 0.05
first_decay = 0.9
second_decay = 0.999
adam_eps = 1e-08
weight_decay = 0.1
update_flags = (False, False, True, False, False, False, False, False, True)

LANES = 128
EDGE = 8
HALO = 2 * EDGE
CHUNK = 16
MIB = 1 << 20

f32 = jnp.float32
bf16 = jnp.bfloat16


def adam_step(weights_now, gradient, moment, square, step_number):
    next_moment = first_decay * moment + (1.0 - first_decay) * gradient
    next_square = second_decay * square + (1.0 - second_decay) * gradient * gradient
    first_fix = 1.0 - jnp.power(jnp.float32(first_decay), step_number)
    second_fix = 1.0 - jnp.power(jnp.float32(second_decay), step_number)
    step_ratio = next_moment / first_fix / (jnp.sqrt(next_square / second_fix) + adam_eps)
    update = -(learn_rate * (step_ratio + weight_decay * weights_now))
    return (weights_now + update, next_moment, next_square, update)


def vmem():
    return pl.BlockSpec(memory_space=pltpu.VMEM)


def smem():
    return pl.BlockSpec(memory_space=pltpu.SMEM)


FAST_MASKS = ((16, 8, 4, 2), (16, 8, 2, 4))


def position(core, dp_rel, x_rel):
    high, low, y = (dp_rel >> 2) & 1, (dp_rel >> 1) & 1, dp_rel & 1
    pair = (y | (x_rel << 1)) if core == 0 else (x_rel | (y << 1))
    return high | (low << 1) | (pair << 2)


def fill_shifted(s, lengths_ref, start, frames_get, left_get, right_get, sh, quarter, width):
    length = lengths_ref[s]
    zeros = jnp.zeros((EDGE, LANES), f32)
    blocks = width // LANES

    def masked(rows, first):
        place = lax.broadcasted_iota(jnp.int32, (rows.shape[0], LANES), 0) + first
        return lambda part: jnp.where(place < length, part, 0.0)

    left, right = left_get().astype(f32), right_get().astype(f32)
    mask_left, mask_right = masked(left, start - EDGE), masked(right, start + quarter)
    for j in range(blocks):
        lane = slice(j * LANES, (j + 1) * LANES)
        sh[j, 0:EDGE, :] = zeros
        sh[j, EDGE : 2 * EDGE, :] = mask_left(left[:, lane])
        sh[j, 2 * EDGE + quarter : 3 * EDGE + quarter, :] = mask_right(right[:, lane])
        sh[j, 3 * EDGE + quarter : 4 * EDGE + quarter, :] = zeros

    def step(i, _):
        row = pl.multiple_of(i * CHUNK, CHUNK)
        part = frames_get(row).astype(f32)
        mask = masked(part, start + row)
        for j in range(blocks):
            sh[j, pl.ds(row + 2 * EDGE, CHUNK), :] = mask(part[:, j * LANES : (j + 1) * LANES])
        return 0

    lax.fori_loop(0, quarter // CHUNK, step, 0)


def front_kernel(slots, quarter, width, taps, ints, frames, cot, left, right, params,
                 normed, unit, inv, bg, normed_t, bg_t, bg_sum, sh):
    half = taps // 2
    blocks = width // LANES
    own_rows = slots * quarter
    start = ints[slots]

    def lanes(j):
        return slice(j * LANES, (j + 1) * LANES)

    def norm_rows(pieces):
        conv = []
        for j in range(blocks):
            parts = []
            for first, rows in pieces:
                acc = jnp.broadcast_to(params[taps : taps + 1, lanes(j)], (rows, LANES))
                for k in range(taps):
                    acc = acc + sh[j, pl.ds(first + k - half, rows), :] * params[k : k + 1, lanes(j)]
                parts.append(acc)
            conv.append(parts[0] if len(parts) == 1 else jnp.concatenate(parts, axis=0))
        total = conv[0]
        for j in range(1, blocks):
            total = total + conv[j]
        mean = jnp.sum(total, axis=1, keepdims=True) * (1.0 / width)
        conv = [c - mean for c in conv]
        total = conv[0] * conv[0]
        for j in range(1, blocks):
            total = total + conv[j] * conv[j]
        inverse = lax.rsqrt(jnp.sum(total, axis=1, keepdims=True) * (1.0 / width) + norm_eps)
        return [c * inverse for c in conv], inverse

    def put_rows(row, pieces):
        parts, inverse = norm_rows(pieces)
        rows = pl.ds(row, CHUNK)
        inv[rows, :] = jnp.broadcast_to(inverse, (CHUNK, LANES))
        for j in range(blocks):
            unit[rows, lanes(j)] = parts[j]
            normed[rows, lanes(j)] = (
                parts[j] * params[taps + 1 : taps + 2, lanes(j)] + params[taps + 2 : taps + 3, lanes(j)]
            ).astype(bf16)

    bg_sum[...] = jnp.zeros_like(bg_sum)
    for s in range(slots):
        length = ints[s]
        fill_shifted(
            s, ints, start,
            lambda row: frames[s, pl.ds(row, CHUNK), :],
            lambda: left[s, 0], lambda: right[s, 0], sh, quarter, width,
        )

        def step(i, _):
            row = pl.multiple_of(i * CHUNK, CHUNK)
            put_rows(pl.multiple_of(s * quarter + row, CHUNK), [(row + 2 * EDGE, CHUNK)])
            place = lax.broadcasted_iota(jnp.int32, (CHUNK, width), 0) + (start + row)
            back = jnp.where(place < length, cot[s, pl.ds(row, CHUNK), :].astype(f32), 0.0)
            low = (back * params[taps + 4 : taps + 5, :]).astype(bf16)
            bg[pl.ds(pl.multiple_of(s * quarter + row, CHUNK), CHUNK), :] = low
            wide = low.astype(f32)
            bg_sum[...] += wide[0:8] + wide[8:16]
            return 0

        lax.fori_loop(0, quarter // CHUNK, step, 0)
        tail = own_rows + s * HALO
        put_rows(tail, [(EDGE, EDGE), (2 * EDGE + quarter, EDGE)])
        edge = jnp.concatenate([left[s, 1].astype(f32), right[s, 1].astype(f32)], axis=0)
        ids = lax.broadcasted_iota(jnp.int32, (HALO, width), 0)
        place = jnp.where(ids < EDGE, start - EDGE + ids, start + quarter - EDGE + ids)
        back = jnp.where(place < length, edge, 0.0)
        bg[tail : tail + HALO, :] = (back * params[taps + 4 : taps + 5, :]).astype(bf16)
        own = slice(s * quarter, (s + 1) * quarter)
        normed_t[:, own] = normed[own, :].T
        bg_t[:, own] = bg[own, :].T


def hidden_kernel(own_rows, row_step, blocks_of, ints, normed, bg, normed_t, bg_t, params, *refs):
    slots, taps, dp_count, own_width, fast = blocks_of
    if fast:
        low_ref, high_ref, refs = refs[0], refs[1], refs[2:]
    else:
        in_up, in_down, refs = refs[0], refs[1], refs[2:]
    act, hg, grads, bias_grad, up, down, hidden, pulled, grad_up, grad_down = refs
    all_rows = normed.shape[0]
    rows_dp = up.shape[0] // dp_count
    dp_own, core = ints[slots + 1], ints[slots + 2]

    def each_block(put):
        for c in range(2):
            @pl.when(core == c)
            def _():
                for dp_rel in range(dp_count):
                    first = pl.multiple_of((dp_rel ^ dp_own) * rows_dp, rows_dp)
                    for x_rel in range(2):
                        put(position(c, dp_rel, x_rel), pl.ds(first, rows_dp), slice(x_rel * own_width, (x_rel + 1) * own_width))

    if fast:
        def gather(place, rows, columns):
            source = (low_ref, high_ref)[place >> 3]
            up[rows, columns] = source[place & 7, :, 0:own_width]
            down[rows, columns] = source[place & 7, :, own_width : 2 * own_width]
        each_block(gather)
    else:
        up[...] = in_up[...]
        down[...] = in_down[...]

    base = taps + 5
    bias = jnp.concatenate(
        [params[pl.ds(base + ints[slots + 3 + x], 1), 0:own_width] for x in range(2)], axis=1
    )
    wide = 2 * own_width
    column_step = 256

    def rows_step(i, _):
        rows = pl.ds(pl.multiple_of(i * row_step, CHUNK), row_step)
        hidden[...] = jnp.dot(normed[rows, :], up[...], preferred_element_type=f32)
        pulled[...] = jnp.dot(bg[rows, :], down[...], preferred_element_type=f32)

        def part(r, _):
            sub = pl.ds(pl.multiple_of(r * CHUNK, CHUNK), CHUNK)
            out = pl.ds(pl.multiple_of(i * row_step + r * CHUNK, CHUNK), CHUNK)
            for column in range(0, wide, column_step):
                columns = slice(column, column + column_step)
                v = hidden[sub, columns] + bias[:, columns]
                fall = jnp.exp(v * v * -0.5)
                t = 1.0 / (1.0 + jnp.abs(v) * (0.3275911 * 0.7071067811865476))
                tail = t * (0.5 * 0.254829592 + t * (0.5 * -0.284496736 + t * (0.5 * 1.421413741 + t * (0.5 * -1.453152027 + t * (0.5 * 1.061405429)))))
                tail = tail * fall
                below = jnp.where(v < 0.0, tail, 1.0 - tail)
                act[out, columns] = (v * below).astype(bf16)
                slope = below + v * (fall * 0.3989422804014327)
                hg[out, columns] = (pulled[sub, columns] * slope).astype(bf16)
            return 0

        lax.fori_loop(0, row_step // CHUNK, part, 0)
        return 0

    lax.fori_loop(0, all_rows // row_step, rows_step, 0)
    grad_up[...] = jnp.dot(normed_t[...], hg[0:own_rows, :], preferred_element_type=f32).astype(grad_up.dtype)
    grad_down[...] = jnp.dot(bg_t[...], act[0:own_rows, :], preferred_element_type=f32).astype(grad_down.dtype)
    bias_grad[...] = jnp.dot(jnp.ones((8, own_rows), bf16), hg[0:own_rows, :], preferred_element_type=f32)
    if fast:
        def scatter(place, rows, columns):
            grads[place, :, 0:own_width] = grad_up[rows, columns]
            grads[place, :, own_width : 2 * own_width] = grad_down[rows, columns]
        each_block(scatter)
    else:
        grads[0] = grad_up[...]
        grads[1] = grad_down[...]


def back_kernel(shape, ints, params, left, right, act0, act1, hg0, hg1, up0, up1, down0, down1, unit, inv, bias0, bias1, bg_sum,
                frames, cot, output, input_grad, small, sh, cgs, ngs, branch, ng_halo, acc):
    slots, quarter, width, taps, own_width = shape
    half = taps // 2
    blocks = width // LANES
    own_rows = slots * quarter
    s = pl.program_id(0)
    start = ints[slots]
    length = ints[s]
    NT = (((1,), (1,)), ((), ()))

    def lanes(j):
        return slice(j * LANES, (j + 1) * LANES)

    def product(a0, a1, w0, w1, rows):
        return lax.dot_general(a0[rows, :], w0[...], NT, preferred_element_type=f32) + lax.dot_general(
            a1[rows, :], w1[...], NT, preferred_element_type=f32
        )

    @pl.when(s == 0)
    def _():
        acc[...] = jnp.zeros_like(acc)
        ng_halo[...] = product(hg0, hg1, up0, up1, pl.ds(own_rows, slots * HALO))

    fill_shifted(
        s, ints, start, lambda row: frames[0, pl.ds(row, CHUNK), :],
        lambda: left[s, 0], lambda: right[s, 0], sh, quarter, width,
    )
    own = pl.ds(pl.multiple_of(s * quarter, CHUNK), quarter)
    ngs[...] = product(hg0, hg1, up0, up1, own)
    branch[...] = product(act0, act1, down0, down1, own)

    def norm_back(ng, rows):
        u = [unit[rows, lanes(j)] for j in range(blocks)]
        scaled = [ng[j] * params[taps + 1 : taps + 2, lanes(j)] for j in range(blocks)]
        first, second = scaled[0], scaled[0] * u[0]
        for j in range(1, blocks):
            first = first + scaled[j]
            second = second + scaled[j] * u[j]
        first = jnp.sum(first, axis=1, keepdims=True) * (1.0 / width)
        second = jnp.sum(second, axis=1, keepdims=True) * (1.0 / width)
        inverse = inv[rows, :]
        return u, [inverse * (scaled[j] - first - u[j] * second) for j in range(blocks)]

    def fold(value):
        return value[0:8] + value[8:16]

    def norm_step(i, _):
        row = pl.multiple_of(i * CHUNK, CHUNK)
        ng = [ngs[pl.ds(row, CHUNK), lanes(j)] for j in range(blocks)]
        u, cg = norm_back(ng, pl.ds(pl.multiple_of(s * quarter + row, CHUNK), CHUNK))
        for j in range(blocks):
            cgs[j, pl.ds(row + 2 * EDGE, CHUNK), :] = cg[j]
            acc[taps + 1, :, lanes(j)] += fold(ng[j] * u[j])
            acc[taps + 2, :, lanes(j)] += fold(ng[j])
            acc[taps, :, lanes(j)] += fold(cg[j])
        return 0

    lax.fori_loop(0, quarter // CHUNK, norm_step, 0)
    tail = pl.multiple_of(s * HALO, HALO)
    ng = [ng_halo[pl.ds(tail, HALO), lanes(j)] for j in range(blocks)]
    _, cg = norm_back(ng, pl.ds(pl.multiple_of(own_rows + tail, HALO), HALO))
    for j in range(blocks):
        cgs[j, 0:EDGE, :] = jnp.zeros((EDGE, LANES), f32)
        cgs[j, EDGE : 2 * EDGE, :] = cg[j][0:EDGE]
        cgs[j, 2 * EDGE + quarter : 3 * EDGE + quarter, :] = cg[j][EDGE:HALO]
        cgs[j, 3 * EDGE + quarter : 4 * EDGE + quarter, :] = jnp.zeros((EDGE, LANES), f32)

    def out_step(i, _):
        row = pl.multiple_of(i * CHUNK, CHUNK)
        rows = pl.ds(row, CHUNK)
        for j in range(blocks):
            place = lax.broadcasted_iota(jnp.int32, (CHUNK, LANES), 0) + (start + row)
            live = place < length
            back = jnp.where(live, cot[0, rows, lanes(j)].astype(f32), 0.0)
            total = branch[rows, lanes(j)] + params[taps + 3 : taps + 4, lanes(j)]
            acc[taps + 4, :, lanes(j)] += fold(back * total)
            shown = frames[0, rows, lanes(j)].astype(f32) + params[taps + 4 : taps + 5, lanes(j)] * total
            output[0, rows, lanes(j)] = jnp.where(live, shown, 0.0)
            first = row + 2 * EDGE
            here = cgs[j, pl.ds(first, CHUNK), :]
            pulled = jnp.zeros((CHUNK, LANES), f32)
            for k in range(taps):
                pulled = pulled + cgs[j, pl.ds(first + half - k, CHUNK), :] * params[k : k + 1, lanes(j)]
                acc[k, :, lanes(j)] += fold(here * sh[j, pl.ds(first + k - half, CHUNK), :])
            input_grad[0, rows, lanes(j)] = back + jnp.where(live, pulled, 0.0)
        return 0

    lax.fori_loop(0, quarter // CHUNK, out_step, 0)

    @pl.when(s == slots - 1)
    def _():
        small[...] = jnp.zeros_like(small)
        for k in range(taps + 3):
            small[k : k + 1, :] = jnp.sum(acc[k], axis=0, keepdims=True)
        small[taps + 3 : taps + 4, :] = jnp.sum(bg_sum[...], axis=0, keepdims=True)
        small[taps + 4 : taps + 5, :] = jnp.sum(acc[taps + 4], axis=0, keepdims=True)
        for n, bias_grad in enumerate((bias0, bias1)):
            for x in range(2):
                place = ints[slots + 3 + 2 * n + x]
                small[pl.ds(taps + 5 + place, 1), 0:own_width] = bias_grad[0:1, x * own_width : (x + 1) * own_width]


def call(kernel, outs, in_specs, scratch, limit, flops=0, moved=0, grid=None, out_specs=None, name=None):
    grid_spec = pltpu.PrefetchScalarGridSpec(
        num_scalar_prefetch=0,
        grid=grid or (),
        in_specs=in_specs,
        out_specs=out_specs or [vmem()] * len(outs),
        scratch_shapes=scratch,
    )
    return pl.pallas_call(
        kernel,
        out_shape=[jax.ShapeDtypeStruct(shape, dtype) for shape, dtype in outs],
        grid_spec=grid_spec,
        compiler_params=pltpu.CompilerParams(vmem_limit_bytes=limit * MIB),
        cost_estimate=pl.CostEstimate(flops=flops, bytes_accessed=moved, transcendentals=0),
        name=name,
    )


def per_device(
    dp_count,
    tp_count,
    frames,
    cotangent,
    lengths,
    conv_weight,
    conv_bias,
    norm_gain,
    norm_bias,
    up_weight,
    up_bias,
    down_weight,
    down_bias,
    layer_scale,
    moment_conv_weight,
    moment_conv_bias,
    moment_norm_gain,
    moment_norm_bias,
    moment_up_weight,
    moment_up_bias,
    moment_down_weight,
    moment_down_bias,
    moment_layer_scale,
    square_conv_weight,
    square_conv_bias,
    square_norm_gain,
    square_norm_bias,
    square_up_weight,
    square_up_bias,
    square_down_weight,
    square_down_bias,
    square_layer_scale,
):
    both = ("dp", "tp")
    count = dp_count * tp_count
    dp_own, tp_own = lax.axis_index("dp"), lax.axis_index("tp")
    own = dp_own * tp_count + tp_own
    slots, quarter, width = frames.shape
    own_channels, taps = conv_weight.shape
    own_bias = up_bias.shape[0]
    own_rows_w, own_width = up_weight.shape
    hidden_width = own_width * tp_count
    all_rows = slots * (quarter + HALO)
    own_rows = slots * quarter
    fast = (dp_count, tp_count) == (8, 4) and own_rows_w % CHUNK == 0
    core = own & 1

    def swap(value, masks):
        return lax.ppermute(value, both, [(i, i ^ masks[i & 1]) for i in range(count)])

    if fast:
        steps = [(FAST_MASKS[0][k], FAST_MASKS[1][k]) for k in range(4)]
        held = jnp.concatenate([up_weight.astype(bf16), down_weight.astype(bf16)], axis=1)[None]
        for k in range(3):
            held = jnp.concatenate([held, swap(held, steps[k])], axis=0)
        far = swap(held, steps[3])
        other = swap(held, (1, 1))
        other_far = swap(far, (1, 1))
        weights = ((held, far), (other, other_far))
        blocks = [[tp_own ^ (2 * x + n) for x in range(2)] for n in range(2)]
    else:
        whole = [
            lax.all_gather(lax.all_gather(w.astype(bf16), "dp", axis=0, tiled=True), "tp", axis=1, tiled=True)
            for w in (up_weight, down_weight)
        ]
        middle = hidden_width // 2
        weights = tuple(tuple(w[:, n * middle : (n + 1) * middle] for w in whole) for n in range(2))
        blocks = [[jnp.int32(2 * n + x) for x in range(2)] for n in range(2)]

    pair = jnp.stack([frames, cotangent], axis=1)
    left = lax.ppermute(pair[:, :, quarter - EDGE :, :], "tp", [(i, i + 1) for i in range(tp_count - 1)])
    right = lax.ppermute(pair[:, :, :EDGE, :], "tp", [(i + 1, i) for i in range(tp_count - 1)])

    small_rows = taps + 5 + tp_count
    channels = jnp.concatenate(
        [conv_weight.T, conv_bias[None], norm_gain[None], norm_bias[None], down_bias[None], layer_scale[None]], axis=0
    )
    params = jnp.zeros((small_rows, width), f32)
    params = lax.dynamic_update_slice(params, channels, (0, own * own_channels))
    params = lax.dynamic_update_slice(
        params, up_bias[None], (taps + 5 + own * own_bias // own_width, own * own_bias % own_width)
    )
    bits = [1 << k for k in range(count.bit_length() - 1)]
    assert 1 << len(bits) == count

    def sum_all(value):
        for bit in bits:
            value = value + swap(value, (bit, bit))
        return value

    params = sum_all(params)

    ints = jnp.stack(
        [*[lengths[s] for s in range(slots)], tp_own * quarter, dp_own, core, *blocks[0], *blocks[1]]
    ).astype(jnp.int32)

    front = call(
        functools.partial(front_kernel, slots, quarter, width, taps),
        [
            ((all_rows, width), bf16),
            ((all_rows, width), f32),
            ((all_rows, LANES), f32),
            ((all_rows, width), bf16),
            ((width, own_rows), bf16),
            ((width, own_rows), bf16),
            ((8, width), f32),
        ],
        [smem(), vmem(), vmem(), vmem(), vmem(), vmem()],
        [pltpu.VMEM((width // LANES, quarter + 4 * EDGE, LANES), f32)],
        16, flops=10 * all_rows * width * taps, moved=8 * all_rows * width, name="front",
    )
    normed, unit, inv, bg, normed_t, bg_t, bg_sum = front(ints, frames, cotangent, left, right, params)

    wide = 2 * own_width
    row_step = 272 if all_rows % 272 == 0 else CHUNK
    results = []
    for n in range(2):
        half_ints = jnp.concatenate(
            [ints[: slots + 2], (ints[slots + 2] ^ n)[None], ints[slots + 3 + 2 * n : slots + 5 + 2 * n]]
        )
        grads_shape = (2 * dp_count, own_rows_w, wide) if fast else (2, width, wide)
        half = call(
            functools.partial(
                hidden_kernel, own_rows, row_step, (slots, taps, dp_count, own_width, fast)
            ),
            [
                ((all_rows, wide), bf16),
                ((all_rows, wide), bf16),
                (grads_shape, bf16 if fast else f32),
                ((8, wide), f32),
                ((width, wide), bf16),
                ((width, wide), bf16),
            ],
            [smem()] + [vmem()] * 7,
            [
                pltpu.VMEM((row_step, wide), f32),
                pltpu.VMEM((row_step, wide), f32),
                pltpu.VMEM((width, wide), bf16 if fast else f32),
                pltpu.VMEM((width, wide), bf16 if fast else f32),
            ],
            24, flops=8 * all_rows * width * wide, moved=8 * all_rows * wide, name=f"hidden{n}",
        )
        results.append(half(half_ints, normed, bg, normed_t, bg_t, params, *weights[n]))
    (act0, hg0, grads0, bias0, up0, down0), (act1, hg1, grads1, bias1, up1, down1) = results

    slot_spec = pl.BlockSpec((1, quarter, width), lambda s: (s, 0, 0))
    back = call(
        functools.partial(back_kernel, (slots, quarter, width, taps, own_width)),
        [
            ((slots, quarter, width), f32),
            ((slots, quarter, width), f32),
            ((small_rows, width), f32),
        ],
        [smem()] + [vmem()] * 16 + [slot_spec, slot_spec],
        [
            pltpu.VMEM((width // LANES, quarter + 4 * EDGE, LANES), f32),
            pltpu.VMEM((width // LANES, quarter + 4 * EDGE, LANES), f32),
            pltpu.VMEM((quarter, width), f32),
            pltpu.VMEM((quarter, width), f32),
            pltpu.VMEM((slots * HALO, width), f32),
            pltpu.VMEM((taps + 5, 8, width), f32),
        ],
        24, flops=4 * all_rows * width * hidden_width, moved=8 * all_rows * width,
        grid=(slots,), out_specs=[slot_spec, slot_spec, vmem()], name="back",
    )
    output_own, input_own, small = back(
        ints, params, left, right, act0, act1, hg0, hg1, up0, up1, down0, down1, unit, inv, bias0, bias1, bg_sum,
        frames, cotangent,
    )

    if fast:
        def plus(a, b):
            return (a.astype(f32) + b.astype(f32)).astype(bf16)

        arrived = swap(grads1, (1, 1))
        keep, send = plus(grads0[:8], arrived[:8]), plus(grads0[8:], arrived[8:])
        for k in range(3, 0, -1):
            size = keep.shape[0] // 2
            arrived = swap(send, steps[k])
            send = plus(keep[size:], arrived[size:])
            keep = plus(keep[:size], arrived[:size])
        arrived = swap(send, steps[0])
        total = keep[0].astype(f32) + arrived[0].astype(f32)
        up_share, down_share = total[:, :own_width], total[:, own_width:]
    else:
        up_share, down_share = (
            lax.psum_scatter(
                lax.psum_scatter(
                    jnp.concatenate([grads0[n], grads1[n]], axis=1), "tp", scatter_dimension=1, tiled=True
                ),
                "dp", scatter_dimension=0, tiled=True,
            )
            for n in range(2)
        )

    small = sum_all(small)
    own_small = lax.dynamic_slice(small, (0, own * own_channels), (taps + 5, own_channels))
    share_up = lax.dynamic_slice(
        small, (taps + 5 + own * own_bias // own_width, own * own_bias % own_width), (1, own_bias)
    )[0]

    step_number = jnp.float32(STEP)
    params_own = (
        conv_weight,
        conv_bias,
        norm_gain,
        norm_bias,
        up_weight,
        up_bias,
        down_weight,
        down_bias,
        layer_scale,
    )
    gradients = (
        own_small[:taps].T,
        own_small[taps],
        own_small[taps + 1],
        own_small[taps + 2],
        up_share,
        share_up,
        down_share,
        own_small[taps + 3],
        own_small[taps + 4],
    )
    moments = (
        moment_conv_weight,
        moment_conv_bias,
        moment_norm_gain,
        moment_norm_bias,
        moment_up_weight,
        moment_up_bias,
        moment_down_weight,
        moment_down_bias,
        moment_layer_scale,
    )
    squares = (
        square_conv_weight,
        square_conv_bias,
        square_norm_gain,
        square_norm_bias,
        square_up_weight,
        square_up_bias,
        square_down_weight,
        square_down_bias,
        square_layer_scale,
    )
    flat = [output_own, input_own]
    for weights_now, gradient, moment, square, use_update in zip(
        params_own, gradients, moments, squares, update_flags
    ):
        next_weights, next_moment, next_square, update = adam_step(
            weights_now, gradient, moment, square, step_number
        )
        shown = update if use_update else next_weights
        flat = flat + [gradient, shown, next_moment, next_square]
    return tuple(flat)


def solution(mesh):
    vector, matrix = P(("dp", "tp")), P("dp", "tp")
    taps = P(("dp", "tp"), None)
    frames = P("dp", "tp", None)
    parameters = (taps, vector, vector, vector, matrix, vector, matrix, vector, vector)
    return jax.shard_map(
        functools.partial(per_device, mesh.shape["dp"], mesh.shape["tp"]),
        mesh=mesh,
        in_specs=(frames, frames, P("dp")) + parameters * 3,
        out_specs=(frames, frames) + tuple(spec for spec in parameters for _ in range(4)),
        check_vma=False,
    )
```

```python
import functools

import jax
import jax.numpy as jnp
from jax import lax
from jax.experimental import pallas as pl
from jax.experimental.pallas import tpu as pltpu
from jax.sharding import PartitionSpec as P


STEP = 4


norm_eps = 1e-06
learn_rate = 0.05
first_decay = 0.9
second_decay = 0.999
adam_eps = 1e-08
weight_decay = 0.1
update_flags = (False, False, True, False, False, False, False, False, True)

LANES = 128
EDGE = 8
HALO = 2 * EDGE
CHUNK = 16
MIB = 1 << 20

f32 = jnp.float32
bf16 = jnp.bfloat16


def adam_step(weights_now, gradient, moment, square, step_number):
    next_moment = first_decay * moment + (1.0 - first_decay) * gradient
    next_square = second_decay * square + (1.0 - second_decay) * gradient * gradient
    first_fix = 1.0 - jnp.power(jnp.float32(first_decay), step_number)
    second_fix = 1.0 - jnp.power(jnp.float32(second_decay), step_number)
    step_ratio = next_moment / first_fix / (jnp.sqrt(next_square / second_fix) + adam_eps)
    update = -(learn_rate * (step_ratio + weight_decay * weights_now))
    return (weights_now + update, next_moment, next_square, update)


def vmem():
    return pl.BlockSpec(memory_space=pltpu.VMEM)


def smem():
    return pl.BlockSpec(memory_space=pltpu.SMEM)


FAST_MASKS = ((16, 8, 4, 2), (16, 8, 2, 4))


def position(core, dp_rel, x_rel):
    high, low, y = (dp_rel >> 2) & 1, (dp_rel >> 1) & 1, dp_rel & 1
    pair = (y | (x_rel << 1)) if core == 0 else (x_rel | (y << 1))
    return high | (low << 1) | (pair << 2)


def fill_shifted(s, lengths_ref, start, frames_get, left_get, right_get, sh, quarter, width):
    length = lengths_ref[s]
    zeros = jnp.zeros((EDGE, LANES), f32)
    blocks = width // LANES

    def masked(rows, first):
        place = lax.broadcasted_iota(jnp.int32, (rows.shape[0], LANES), 0) + first
        return lambda part: jnp.where(place < length, part, 0.0)

    left, right = left_get().astype(f32), right_get().astype(f32)
    mask_left, mask_right = masked(left, start - EDGE), masked(right, start + quarter)
    for j in range(blocks):
        lane = slice(j * LANES, (j + 1) * LANES)
        sh[j, 0:EDGE, :] = zeros
        sh[j, EDGE : 2 * EDGE, :] = mask_left(left[:, lane])
        sh[j, 2 * EDGE + quarter : 3 * EDGE + quarter, :] = mask_right(right[:, lane])
        sh[j, 3 * EDGE + quarter : 4 * EDGE + quarter, :] = zeros

    def step(i, _):
        row = pl.multiple_of(i * CHUNK, CHUNK)
        part = frames_get(row).astype(f32)
        mask = masked(part, start + row)
        for j in range(blocks):
            sh[j, pl.ds(row + 2 * EDGE, CHUNK), :] = mask(part[:, j * LANES : (j + 1) * LANES])
        return 0

    lax.fori_loop(0, quarter // CHUNK, step, 0)


GROUP = 4


def front_kernel(slots, quarter, width, taps, ints, frames, cot, left, right, params,
                 normed, unit, bg, normed_t, bg_t, bg_sum, sh):
    half = taps // 2
    blocks = width // LANES
    own_rows = slots * quarter
    start = ints[slots]

    def lanes(j):
        return slice(j * LANES, (j + 1) * LANES)

    def put_rows(chunks):
        conv = []
        for _, pieces in chunks:
            conv.append([])
            for j in range(blocks):
                parts = []
                for first, rows in pieces:
                    acc = jnp.broadcast_to(params[taps : taps + 1, lanes(j)], (rows, LANES))
                    for k in range(taps):
                        acc = acc + sh[j, pl.ds(first + k - half, rows), :] * params[k : k + 1, lanes(j)]
                    parts.append(acc)
                conv[-1].append(parts[0] if len(parts) == 1 else jnp.concatenate(parts, axis=0))
        means = [jnp.sum(functools.reduce(jnp.add, c), axis=1, keepdims=True) * (1.0 / width) for c in conv]
        conv = [[part - mean for part in c] for c, mean in zip(conv, means)]
        spread = [
            jnp.sum(functools.reduce(jnp.add, [part * part for part in c]), axis=1, keepdims=True) * (1.0 / width)
            for c in conv
        ]
        inverses = [lax.rsqrt(v + norm_eps) for v in spread]
        for (row, _), c, inverse in zip(chunks, conv, inverses):
            rows = pl.ds(row, CHUNK)
            unit[rows, lanes(blocks)] = jnp.broadcast_to(inverse, (CHUNK, LANES))
            for j in range(blocks):
                part = c[j] * inverse
                unit[rows, lanes(j)] = part
                normed[rows, lanes(j)] = (
                    part * params[taps + 1 : taps + 2, lanes(j)] + params[taps + 2 : taps + 3, lanes(j)]
                ).astype(bf16)

    bg_sum[...] = jnp.zeros_like(bg_sum)
    for s in range(slots):
        length = ints[s]
        fill_shifted(
            s, ints, start,
            lambda row: frames[s, pl.ds(row, CHUNK), :],
            lambda: left[s, 0], lambda: right[s, 0], sh, quarter, width,
        )

        def step(i, _):
            chunks = []
            for u in range(GROUP):
                row = pl.multiple_of(i * (GROUP * CHUNK) + u * CHUNK, CHUNK)
                chunks.append((pl.multiple_of(s * quarter + row, CHUNK), [(row + 2 * EDGE, CHUNK)]))
            put_rows(chunks)
            total = None
            for u in range(GROUP):
                row = pl.multiple_of(i * (GROUP * CHUNK) + u * CHUNK, CHUNK)
                place = lax.broadcasted_iota(jnp.int32, (CHUNK, width), 0) + (start + row)
                back = jnp.where(place < length, cot[s, pl.ds(row, CHUNK), :].astype(f32), 0.0)
                low = (back * params[taps + 4 : taps + 5, :]).astype(bf16)
                bg[pl.ds(pl.multiple_of(s * quarter + row, CHUNK), CHUNK), :] = low
                wide = low.astype(f32)
                wide = wide[0:8] + wide[8:16]
                total = wide if total is None else total + wide
            bg_sum[...] += total
            return 0

        lax.fori_loop(0, quarter // (GROUP * CHUNK), step, 0)
        tail = own_rows + s * HALO
        put_rows([(tail, [(EDGE, EDGE), (2 * EDGE + quarter, EDGE)])])
        edge = jnp.concatenate([left[s, 1].astype(f32), right[s, 1].astype(f32)], axis=0)
        ids = lax.broadcasted_iota(jnp.int32, (HALO, width), 0)
        place = jnp.where(ids < EDGE, start - EDGE + ids, start + quarter - EDGE + ids)
        back = jnp.where(place < length, edge, 0.0)
        bg[tail : tail + HALO, :] = (back * params[taps + 4 : taps + 5, :]).astype(bf16)
        own = slice(s * quarter, (s + 1) * quarter)
        normed_t[:, own] = normed[own, :].T
        bg_t[:, own] = bg[own, :].T


TILE = 256


def hidden_kernel(slots, taps, dp_count, own_width, own_rows, fast, ints, normed, bg, normed_t, bg_t, params, *refs):
    sources, refs = (refs[:4], refs[4:]) if fast else (refs[:2], refs[2:])
    act, hg, *grads, bias_grad, up, down, hid_a, hid_b, pull_a, pull_b = refs
    all_rows, width = normed.shape
    wide = 2 * own_width
    rows_dp = width // dp_count
    dp_own, core = ints[slots + 1], ints[slots + 2]

    if fast:
        for n in range(2):
            for c in range(2):
                @pl.when(core == c)
                def _():
                    for dp_rel in range(dp_count):
                        rows = pl.ds(pl.multiple_of((dp_rel ^ dp_own) * rows_dp, rows_dp), rows_dp)
                        for x_rel in range(2):
                            place = position(c ^ n, dp_rel, x_rel)
                            source = sources[2 * n + (place >> 3)]
                            columns = slice(n * wide + x_rel * own_width, n * wide + (x_rel + 1) * own_width)
                            up[rows, columns] = source[place & 7, :, 0:own_width]
                            down[rows, columns] = source[place & 7, :, own_width : 2 * own_width]
    else:
        up[...] = sources[0][...]
        down[...] = sources[1][...]

    base = taps + 5
    bias = [
        jnp.concatenate(
            [params[pl.ds(base + ints[slots + 3 + 2 * n + x], 1), 0:own_width] for x in range(2)], axis=1
        )
        for n in range(2)
    ]
    thirds = [slice(k * (own_rows // 3), (k + 1) * (own_rows // 3)) for k in range(3)]
    thirds[2] = slice(thirds[2].start, all_rows)
    stages = [(n, rows) for n in (1, 0) for rows in thirds]

    def products(k):
        n, rows = stages[k]
        count = rows.stop - rows.start
        hid, pull = ((hid_a, pull_a), (hid_b, pull_b))[k % 2]

        def one(out, left, right, column):
            columns = slice(n * wide + column, n * wide + column + TILE)
            out[0:count, column : column + TILE] = jnp.dot(left[rows, :], right[:, columns], preferred_element_type=f32)

        return [
            functools.partial(one, out, left, right, column)
            for column in range(0, wide, TILE)
            for out, left, right in ((hid, normed, up), (pull, bg, down))
        ]

    def elementwise(k):
        n, rows = stages[k]
        count = rows.stop - rows.start
        hid, pull = ((hid_a, pull_a), (hid_b, pull_b))[k % 2]

        def one(sub, column):
            source = (slice(sub, sub + CHUNK), slice(column, column + TILE))
            first = rows.start + sub
            place = (slice(first, first + CHUNK), slice(n * wide + column, n * wide + column + TILE))
            v = hid[source] + bias[n][:, column : column + TILE]
            fall = jnp.exp2(v * v * (-0.5 * 1.4426950408889634))
            t = 1.0 / (1.0 + jnp.abs(v) * (0.3275911 * 0.7071067811865476))
            tail = 0.5 * -1.453152027 + t * (0.5 * 1.061405429)
            tail = 0.5 * 1.421413741 + t * tail
            tail = 0.5 * -0.284496736 + t * tail
            tail = 0.5 * 0.254829592 + t * tail
            tail = t * tail * fall
            below = jnp.where(v < 0.0, tail, 1.0 - tail)
            if first < own_rows:
                act[place] = (v * below).astype(bf16)
            slope = below + v * (fall * 0.3989422804014327)
            hg[place] = (pull[source] * slope).astype(bf16)

        return [
            functools.partial(one, sub, column) for column in range(0, wide, TILE) for sub in range(0, count, CHUNK)
        ]

    def weight_grads(n):
        def one(which, row, column):
            columns = slice(n * wide + column, n * wide + column + TILE)
            left, right = ((normed_t, hg), (bg_t, act))[which]
            value = jnp.dot(left[row : row + TILE, :], right[0:own_rows, columns], preferred_element_type=f32)
            if not fast:
                grads[0][which, row : row + TILE, columns] = value
                return
            value = value.astype(bf16)
            for dp in range(row // rows_dp, (row + TILE) // rows_dp):
                dp_rel = dp ^ dp_own
                high, low, y = (dp_rel >> 2) & 1, (dp_rel >> 1) & 1, dp_rel & 1
                owner = core ^ n
                for x in range(2):
                    first, last = max(column, x * own_width), min(column + TILE, (x + 1) * own_width)
                    if first >= last:
                        continue
                    place = high + 2 * low + 4 * (y * (1 + owner) + x * (2 - owner))
                    out = slice(which * own_width + first - x * own_width, which * own_width + last - x * own_width)
                    grads[n][place, :, out] = value[
                        dp * rows_dp - row : (dp + 1) * rows_dp - row, first - column : last - column
                    ]

        def sums():
            columns = slice(n * wide, (n + 1) * wide)
            bias_grad[:, columns] = jnp.dot(
                jnp.ones((8, own_rows), bf16), hg[0:own_rows, columns], preferred_element_type=f32
            )

        pieces = [
            functools.partial(one, which, row, column)
            for column in range(0, wide, TILE)
            for which in range(2)
            for row in range(0, width, TILE)
        ]
        return pieces + [sums]

    def run(matrix, vector):
        done = 0
        for k, piece in enumerate(matrix):
            piece()
            upto = len(vector) * (k + 1) // len(matrix)
            for other in vector[done:upto]:
                other()
            done = upto

    run(products(0), [])
    run(products(1), elementwise(0))
    run(products(2), elementwise(1))
    run(products(3), elementwise(2))
    grads_1 = weight_grads(1)
    run(products(4) + grads_1[:6], elementwise(3))
    run(products(5) + grads_1[6:], elementwise(4))
    for piece in elementwise(5):
        piece()
    run(weight_grads(0), [])


NT = (((1,), (1,)), ((), ()))


def output_kernel(slots, quarter, width, taps, ints, params, act, down, frames, cot, output, scale_sum, branch):
    s = pl.program_id(0)
    start, length = ints[slots], ints[s]

    @pl.when(s == 0)
    def _():
        scale_sum[...] = jnp.zeros_like(scale_sum)

    own = pl.ds(pl.multiple_of(s * quarter, CHUNK), quarter)
    branch[...] = lax.dot_general(act[own, :], down[...], NT, preferred_element_type=f32)

    def step(i, total_sum):
        row = pl.multiple_of(i * CHUNK, CHUNK)
        rows = pl.ds(row, CHUNK)
        live = lax.broadcasted_iota(jnp.int32, (CHUNK, width), 0) + (start + row) < length
        back = jnp.where(live, cot[0, rows, :].astype(f32), 0.0)
        total = branch[rows, :] + params[taps + 3 : taps + 4, :]
        shown = frames[0, rows, :].astype(f32) + params[taps + 4 : taps + 5, :] * total
        output[0, rows, :] = jnp.where(live, shown, 0.0)
        part = back * total
        return total_sum + (part[0:8] + part[8:16])

    scale_sum[...] += lax.fori_loop(0, quarter // CHUNK, step, jnp.zeros((8, width), f32))


def back_kernel(shape, ints, params, left, right, hg, up, unit, bias_grad, bg_sum, scale_sum,
                frames, cot, input_grad, small, sh, cgs, ngs, ng_halo, acc):
    slots, quarter, width, taps, own_width = shape
    half = taps // 2
    blocks = width // LANES
    own_rows = slots * quarter
    s = pl.program_id(0)
    start = ints[slots]
    length = ints[s]

    def lanes(j):
        return slice(j * LANES, (j + 1) * LANES)

    def product(rows):
        return lax.dot_general(hg[rows, :], up[...], NT, preferred_element_type=f32)

    @pl.when(s == 0)
    def _():
        acc[...] = jnp.zeros_like(acc)
        ng_halo[...] = product(pl.ds(own_rows, slots * HALO))

    fill_shifted(
        s, ints, start, lambda row: frames[0, pl.ds(row, CHUNK), :],
        lambda: left[s, 0], lambda: right[s, 0], sh, quarter, width,
    )
    ngs[...] = product(pl.ds(pl.multiple_of(s * quarter, CHUNK), quarter))

    def norm_back(chunks):
        units, scales, firsts, seconds = [], [], [], []
        for ng, rows in chunks:
            u = [unit[rows, lanes(j)] for j in range(blocks)]
            scaled = [ng[j] * params[taps + 1 : taps + 2, lanes(j)] for j in range(blocks)]
            units.append(u)
            scales.append(scaled)
            firsts.append(functools.reduce(jnp.add, scaled))
            seconds.append(functools.reduce(jnp.add, [a * b for a, b in zip(scaled, u)]))
        firsts = [jnp.sum(v, axis=1, keepdims=True) * (1.0 / width) for v in firsts]
        seconds = [jnp.sum(v, axis=1, keepdims=True) * (1.0 / width) for v in seconds]
        grads = []
        for (_, rows), u, scaled, first, second in zip(chunks, units, scales, firsts, seconds):
            inverse = unit[rows, lanes(blocks)]
            grads.append([inverse * (scaled[j] - first - u[j] * second) for j in range(blocks)])
        return units, grads

    def fold(value):
        return value[0:8] + value[8:16]

    def norm_step(i, _):
        firsts = [pl.multiple_of(i * (2 * CHUNK) + u * CHUNK, CHUNK) for u in range(2)]
        ngs_here = [[ngs[pl.ds(row, CHUNK), lanes(j)] for j in range(blocks)] for row in firsts]
        units, grads = norm_back(
            [(ng, pl.ds(pl.multiple_of(s * quarter + row, CHUNK), CHUNK)) for ng, row in zip(ngs_here, firsts)]
        )
        for j in range(blocks):
            for row, cg in zip(firsts, grads):
                cgs[j, pl.ds(row + 2 * EDGE, CHUNK), :] = cg[j]
            acc[taps + 1, :, lanes(j)] += functools.reduce(jnp.add, [fold(ng[j] * u[j]) for ng, u in zip(ngs_here, units)])
            acc[taps + 2, :, lanes(j)] += functools.reduce(jnp.add, [fold(ng[j]) for ng in ngs_here])
            acc[taps, :, lanes(j)] += functools.reduce(jnp.add, [fold(cg[j]) for cg in grads])
        return 0

    lax.fori_loop(0, quarter // (2 * CHUNK), norm_step, 0)
    tail = pl.multiple_of(s * HALO, HALO)
    ng = [ng_halo[pl.ds(tail, HALO), lanes(j)] for j in range(blocks)]
    _, (cg,) = norm_back([(ng, pl.ds(pl.multiple_of(own_rows + tail, HALO), HALO))])
    for j in range(blocks):
        cgs[j, 0:EDGE, :] = jnp.zeros((EDGE, LANES), f32)
        cgs[j, EDGE : 2 * EDGE, :] = cg[j][0:EDGE]
        cgs[j, 2 * EDGE + quarter : 3 * EDGE + quarter, :] = cg[j][EDGE:HALO]
        cgs[j, 3 * EDGE + quarter : 4 * EDGE + quarter, :] = jnp.zeros((EDGE, LANES), f32)

    for j in range(blocks):
        def conv_step(i, sums):
            row = pl.multiple_of(i * CHUNK, CHUNK)
            rows = pl.ds(row, CHUNK)
            live = lax.broadcasted_iota(jnp.int32, (CHUNK, LANES), 0) + (start + row) < length
            back = jnp.where(live, cot[0, rows, lanes(j)].astype(f32), 0.0)
            first = row + 2 * EDGE
            here = cgs[j, pl.ds(first, CHUNK), :]
            pulled = jnp.zeros((CHUNK, LANES), f32)
            out = []
            for k in range(taps):
                pulled = pulled + cgs[j, pl.ds(first + half - k, CHUNK), :] * params[k : k + 1, lanes(j)]
                out.append(sums[k] + fold(here * sh[j, pl.ds(first + k - half, CHUNK), :]))
            input_grad[0, rows, lanes(j)] = back + jnp.where(live, pulled, 0.0)
            return tuple(out)

        sums = lax.fori_loop(
            0, quarter // CHUNK, conv_step, tuple(jnp.zeros((8, LANES), f32) for _ in range(taps))
        )
        for k in range(taps):
            acc[k, :, lanes(j)] += sums[k]

    @pl.when(s == slots - 1)
    def _():
        small[...] = jnp.zeros_like(small)
        for k in range(taps + 3):
            small[k : k + 1, :] = jnp.sum(acc[k], axis=0, keepdims=True)
        small[taps + 3 : taps + 4, :] = jnp.sum(bg_sum[...], axis=0, keepdims=True)
        small[taps + 4 : taps + 5, :] = jnp.sum(scale_sum[...], axis=0, keepdims=True)
        for x in range(4):
            place = ints[slots + 3 + x]
            small[pl.ds(taps + 5 + place, 1), 0:own_width] = bias_grad[0:1, x * own_width : (x + 1) * own_width]


def call(kernel, outs, in_specs, scratch, limit, flops=0, moved=0, grid=None, out_specs=None):
    grid_spec = pltpu.PrefetchScalarGridSpec(
        num_scalar_prefetch=0,
        grid=grid or (),
        in_specs=in_specs,
        out_specs=out_specs or [vmem()] * len(outs),
        scratch_shapes=scratch,
    )
    return pl.pallas_call(
        kernel,
        out_shape=[jax.ShapeDtypeStruct(shape, dtype) for shape, dtype in outs],
        grid_spec=grid_spec,
        compiler_params=pltpu.CompilerParams(vmem_limit_bytes=limit * MIB),
        cost_estimate=pl.CostEstimate(flops=flops, bytes_accessed=moved, transcendentals=0),
    )


def per_device(
    dp_count,
    tp_count,
    frames,
    cotangent,
    lengths,
    conv_weight,
    conv_bias,
    norm_gain,
    norm_bias,
    up_weight,
    up_bias,
    down_weight,
    down_bias,
    layer_scale,
    moment_conv_weight,
    moment_conv_bias,
    moment_norm_gain,
    moment_norm_bias,
    moment_up_weight,
    moment_up_bias,
    moment_down_weight,
    moment_down_bias,
    moment_layer_scale,
    square_conv_weight,
    square_conv_bias,
    square_norm_gain,
    square_norm_bias,
    square_up_weight,
    square_up_bias,
    square_down_weight,
    square_down_bias,
    square_layer_scale,
):
    both = ("dp", "tp")
    count = dp_count * tp_count
    dp_own, tp_own = lax.axis_index("dp"), lax.axis_index("tp")
    own = dp_own * tp_count + tp_own
    slots, quarter, width = frames.shape
    own_channels, taps = conv_weight.shape
    own_bias = up_bias.shape[0]
    own_rows_w, own_width = up_weight.shape
    hidden_width = own_width * tp_count
    all_rows = slots * (quarter + HALO)
    own_rows = slots * quarter
    fast = (dp_count, tp_count) == (8, 4) and own_rows_w % CHUNK == 0
    core = own & 1

    def swap(value, masks):
        return lax.ppermute(value, both, [(i, i ^ masks[i & 1]) for i in range(count)])

    if fast:
        steps = [(FAST_MASKS[0][k], FAST_MASKS[1][k]) for k in range(4)]
        held = jnp.concatenate([up_weight.astype(bf16), down_weight.astype(bf16)], axis=1)[None]
        for k in range(3):
            arrived = swap(held, steps[k])
            held = jnp.concatenate([held, arrived], axis=0)
        far = swap(held, steps[3])
        other = swap(held, (1, 1))
        other_far = swap(far, (1, 1))
        weights = (held, far, other, other_far)
        blocks = [[tp_own ^ (2 * x + n) for x in range(2)] for n in range(2)]
    else:
        weights = [
            lax.all_gather(lax.all_gather(w.astype(bf16), "dp", axis=0, tiled=True), "tp", axis=1, tiled=True)
            for w in (up_weight, down_weight)
        ]
        blocks = [[jnp.int32(2 * n + x) for x in range(2)] for n in range(2)]

    pair = jnp.stack([frames, cotangent], axis=1)
    left = lax.ppermute(pair[:, :, quarter - EDGE :, :], "tp", [(i, i + 1) for i in range(tp_count - 1)])
    right = lax.ppermute(pair[:, :, :EDGE, :], "tp", [(i + 1, i) for i in range(tp_count - 1)])

    small_rows = taps + 5 + tp_count
    channels = jnp.concatenate(
        [conv_weight.T, conv_bias[None], norm_gain[None], norm_bias[None], down_bias[None], layer_scale[None]], axis=0
    )
    params = jnp.zeros((small_rows, width), f32)
    params = lax.dynamic_update_slice(params, channels, (0, own * own_channels))
    params = lax.dynamic_update_slice(
        params, up_bias[None], (taps + 5 + own * own_bias // own_width, own * own_bias % own_width)
    )
    bits = [1 << k for k in range(count.bit_length() - 1)]
    assert 1 << len(bits) == count

    def sum_all(value, order):
        for bit in order:
            arrived = swap(value, (bit, bit))
            value = value + arrived
        return value

    params = sum_all(params, bits)

    ints = jnp.stack(
        [*[lengths[s] for s in range(slots)], tp_own * quarter, dp_own, core, *blocks[0], *blocks[1]]
    ).astype(jnp.int32)

    front = call(
        functools.partial(front_kernel, slots, quarter, width, taps),
        [
            ((all_rows, width), bf16),
            ((all_rows, width + LANES), f32),
            ((all_rows, width), bf16),
            ((width, own_rows), bf16),
            ((width, own_rows), bf16),
            ((8, width), f32),
        ],
        [smem(), vmem(), vmem(), vmem(), vmem(), vmem()],
        [pltpu.VMEM((width // LANES, quarter + 4 * EDGE, LANES), f32)],
        4, flops=10 * all_rows * width * taps, moved=8 * all_rows * width,
    )
    normed, unit, bg, normed_t, bg_t, bg_sum = front(ints, frames, cotangent, left, right, params)

    wide = 2 * own_width
    grads_shape = (2 * dp_count, own_rows_w, wide)
    most = own_rows // 3 + all_rows - own_rows
    hidden = call(
        functools.partial(hidden_kernel, slots, taps, dp_count, own_width, own_rows, fast),
        [((own_rows, hidden_width), bf16), ((all_rows, hidden_width), bf16)]
        + ([(grads_shape, bf16)] * 2 if fast else [((2, width, hidden_width), f32)])
        + [((8, hidden_width), f32), ((width, hidden_width), bf16), ((width, hidden_width), bf16)],
        [smem()] + [vmem()] * (5 + len(weights)),
        [pltpu.VMEM((most, wide), f32)] * 4,
        10, flops=8 * all_rows * width * hidden_width, moved=8 * all_rows * hidden_width,
    )
    act, hg, *grads, bias_grad, up, down = hidden(ints, normed, bg, normed_t, bg_t, params, *weights)

    slot_spec = pl.BlockSpec((1, quarter, width), lambda s: (s, 0, 0))
    output = call(
        functools.partial(output_kernel, slots, quarter, width, taps),
        [((slots, quarter, width), f32), ((8, width), f32)],
        [smem(), vmem(), vmem(), vmem(), slot_spec, slot_spec],
        [pltpu.VMEM((quarter, width), f32)],
        8, flops=2 * own_rows * width * hidden_width, moved=8 * all_rows * width,
        grid=(slots,), out_specs=[slot_spec, vmem()],
    )
    output_own, scale_sum = output(ints, params, act, down, frames, cotangent)
    back = call(
        functools.partial(back_kernel, (slots, quarter, width, taps, own_width)),
        [((slots, quarter, width), f32), ((small_rows, width), f32)],
        [smem()] + [vmem()] * 9 + [slot_spec, slot_spec],
        [
            pltpu.VMEM((width // LANES, quarter + 4 * EDGE, LANES), f32),
            pltpu.VMEM((width // LANES, quarter + 4 * EDGE, LANES), f32),
            pltpu.VMEM((quarter, width), f32),
            pltpu.VMEM((slots * HALO, width), f32),
            pltpu.VMEM((taps + 5, 8, width), f32),
        ],
        8, flops=2 * all_rows * width * hidden_width, moved=8 * all_rows * width,
        grid=(slots,), out_specs=[slot_spec, vmem()],
    )
    input_own, small = back(ints, params, left, right, hg, up, unit, bias_grad, bg_sum, scale_sum, frames, cotangent)

    if fast:
        def plus(a, b):
            return (a.astype(f32) + b.astype(f32)).astype(bf16)

        arrived = swap(grads[1], (1, 1))
        keep, send = plus(grads[0][:8], arrived[:8]), plus(grads[0][8:], arrived[8:])
        for k in range(3, 0, -1):
            size = keep.shape[0] // 2
            arrived = swap(send, steps[k])
            send = plus(keep[size:], arrived[size:])
            keep = plus(keep[:size], arrived[:size])
        arrived = swap(send, steps[0])
        total = keep[0].astype(f32) + arrived[0].astype(f32)
        up_share, down_share = total[:, :own_width], total[:, own_width:]
    else:
        up_share, down_share = (
            lax.psum_scatter(
                lax.psum_scatter(grads[0][n], "tp", scatter_dimension=1, tiled=True),
                "dp", scatter_dimension=0, tiled=True,
            )
            for n in range(2)
        )

    small = sum_all(small, (1, 8, 2, 4, 16) if fast else bits)
    own_small = lax.dynamic_slice(small, (0, own * own_channels), (taps + 5, own_channels))
    share_up = lax.dynamic_slice(
        small, (taps + 5 + own * own_bias // own_width, own * own_bias % own_width), (1, own_bias)
    )[0]

    step_number = jnp.float32(STEP)
    params_own = (
        conv_weight,
        conv_bias,
        norm_gain,
        norm_bias,
        up_weight,
        up_bias,
        down_weight,
        down_bias,
        layer_scale,
    )
    gradients = (
        own_small[:taps].T,
        own_small[taps],
        own_small[taps + 1],
        own_small[taps + 2],
        up_share,
        share_up,
        down_share,
        own_small[taps + 3],
        own_small[taps + 4],
    )
    moments = (
        moment_conv_weight,
        moment_conv_bias,
        moment_norm_gain,
        moment_norm_bias,
        moment_up_weight,
        moment_up_bias,
        moment_down_weight,
        moment_down_bias,
        moment_layer_scale,
    )
    squares = (
        square_conv_weight,
        square_conv_bias,
        square_norm_gain,
        square_norm_bias,
        square_up_weight,
        square_up_bias,
        square_down_weight,
        square_down_bias,
        square_layer_scale,
    )
    flat = [output_own, input_own]
    for weights_now, gradient, moment, square, use_update in zip(
        params_own, gradients, moments, squares, update_flags
    ):
        next_weights, next_moment, next_square, update = adam_step(
            weights_now, gradient, moment, square, step_number
        )
        shown = update if use_update else next_weights
        flat = flat + [gradient, shown, next_moment, next_square]
    return tuple(flat)


def body(dp_count, tp_count, *args):
    return per_device(dp_count, tp_count, *args)


def solution(mesh):
    vector, matrix = P(("dp", "tp")), P("dp", "tp")
    taps = P(("dp", "tp"), None)
    frames = P("dp", "tp", None)
    parameters = (taps, vector, vector, vector, matrix, vector, matrix, vector, vector)
    return jax.shard_map(
        functools.partial(body, mesh.shape["dp"], mesh.shape["tp"]),
        mesh=mesh,
        in_specs=(frames, frames, P("dp")) + parameters * 3,
        out_specs=(frames, frames) + tuple(spec for spec in parameters for _ in range(4)),
        check_vma=False,
    )
```

```python
import functools

import jax
import jax.numpy as jnp
from jax import lax
from jax.experimental import pallas as pl
from jax.experimental.pallas import tpu as pltpu
from jax.sharding import PartitionSpec as P


STEP = 4


norm_eps = 1e-06
learn_rate = 0.05
first_decay = 0.9
second_decay = 0.999
adam_eps = 1e-08
weight_decay = 0.1
update_flags = (False, False, True, False, False, False, False, False, True)

LANES = 128
EDGE = 8
HALO = 2 * EDGE
CHUNK = 16
MIB = 1 << 20

f32 = jnp.float32
bf16 = jnp.bfloat16


def adam_step(weights_now, gradient, moment, square, step_number):
    next_moment = first_decay * moment + (1.0 - first_decay) * gradient
    next_square = second_decay * square + (1.0 - second_decay) * gradient * gradient
    if step_number is None:
        first_fix, second_fix = 1.0 - first_decay**STEP, 1.0 - second_decay**STEP
    else:
        first_fix = 1.0 - jnp.power(jnp.float32(first_decay), step_number)
        second_fix = 1.0 - jnp.power(jnp.float32(second_decay), step_number)
    step_ratio = next_moment / first_fix / (jnp.sqrt(next_square / second_fix) + adam_eps)
    update = -(learn_rate * (step_ratio + weight_decay * weights_now))
    return (weights_now + update, next_moment, next_square, update)


def vmem():
    return pl.BlockSpec(memory_space=pltpu.VMEM)


def whole(shape):
    return pl.BlockSpec(shape, lambda: (0,) * len(shape))


def smem():
    return pl.BlockSpec(memory_space=pltpu.SMEM)


FAST_MASKS = ((16, 8, 4, 2), (8, 16, 2, 4))

FEW_ORDER = ((1, 1), (4, 2), (2, 4), (8, 8), (16, 16))
SUM_ORDER = ((1, 1), (16, 16), (2, 4), (4, 2), (8, 8))


def position(core, dp_rel, x_rel):
    high, low, y = (dp_rel >> 2) & 1, (dp_rel >> 1) & 1, dp_rel & 1
    if core == 0:
        return high | (low << 1) | (y << 2) | (x_rel << 3)
    return low | (high << 1) | (x_rel << 2) | (y << 3)


def fill_shifted(s, lengths_ref, start, frames_get, left_get, right_get, sh, quarter, width):
    length = lengths_ref[s]
    zeros = jnp.zeros((EDGE, LANES), f32)
    blocks = width // LANES

    def masked(rows, first):
        place = lax.broadcasted_iota(jnp.int32, (rows.shape[0], LANES), 0) + first
        return lambda part: jnp.where(place < length, part, 0.0)

    left, right = left_get().astype(f32), right_get().astype(f32)
    mask_left, mask_right = masked(left, start - EDGE), masked(right, start + quarter)
    for j in range(blocks):
        lane = slice(j * LANES, (j + 1) * LANES)
        sh[j, 0:EDGE, :] = zeros
        sh[j, EDGE : 2 * EDGE, :] = mask_left(left[:, lane])
        sh[j, 2 * EDGE + quarter : 3 * EDGE + quarter, :] = mask_right(right[:, lane])
        sh[j, 3 * EDGE + quarter : 4 * EDGE + quarter, :] = zeros

    def step(i, _):
        row = pl.multiple_of(i * CHUNK, CHUNK)
        part = frames_get(row).astype(f32)
        mask = masked(part, start + row)
        for j in range(blocks):
            sh[j, pl.ds(row + 2 * EDGE, CHUNK), :] = mask(part[:, j * LANES : (j + 1) * LANES])
        return 0

    lax.fori_loop(0, quarter // CHUNK, step, 0)


GROUP = 4
STRIDE = 64


def front_kernel(slots, quarter, width, taps, ints, frames, cot, left, right, params,
                 normed, unit, bg, normed_t, bg_t, bg_sum, sh):
    half = taps // 2
    blocks = width // LANES
    own_rows = slots * quarter
    start = ints[slots]

    def lanes(j):
        return slice(j * LANES, (j + 1) * LANES)

    def put_rows(chunks):
        conv = []
        for _, pieces in chunks:
            conv.append([])
            for j in range(blocks):
                parts = []
                for first, rows in pieces:
                    acc = jnp.broadcast_to(params[taps : taps + 1, lanes(j)], (rows, LANES))
                    for k in range(taps):
                        acc = acc + sh[j, pl.ds(first + k - half, rows), :] * params[k : k + 1, lanes(j)]
                    parts.append(acc)
                conv[-1].append(parts[0] if len(parts) == 1 else jnp.concatenate(parts, axis=0))
        means = [jnp.sum(functools.reduce(jnp.add, c), axis=1, keepdims=True) * (1.0 / width) for c in conv]
        conv = [[part - mean for part in c] for c, mean in zip(conv, means)]
        spread = [
            jnp.sum(functools.reduce(jnp.add, [part * part for part in c]), axis=1, keepdims=True) * (1.0 / width)
            for c in conv
        ]
        inverses = [lax.rsqrt(v + norm_eps) for v in spread]
        for (row, _), c, inverse in zip(chunks, conv, inverses):
            rows = pl.ds(row, CHUNK)
            unit[rows, lanes(blocks)] = jnp.broadcast_to(inverse, (CHUNK, LANES))
            for j in range(blocks):
                part = c[j] * inverse
                unit[rows, lanes(j)] = part
                normed[rows, lanes(j)] = (
                    part * params[taps + 1 : taps + 2, lanes(j)] + params[taps + 2 : taps + 3, lanes(j)]
                ).astype(bf16)

    bg_sum[...] = jnp.zeros_like(bg_sum)
    for s in range(slots):
        length = ints[s]
        fill_shifted(
            s, ints, start,
            lambda row: frames[s, pl.ds(row, CHUNK), :],
            lambda: left[s, 0], lambda: right[s, 0], sh, quarter, width,
        )

        def step(i, _):
            chunks = []
            for u in range(GROUP):
                row = pl.multiple_of(i * (GROUP * CHUNK) + u * CHUNK, CHUNK)
                chunks.append((pl.multiple_of(s * quarter + row, CHUNK), [(row + 2 * EDGE, CHUNK)]))
            put_rows(chunks)
            total = None
            for u in range(GROUP):
                row = pl.multiple_of(i * (GROUP * CHUNK) + u * CHUNK, CHUNK)
                place = lax.broadcasted_iota(jnp.int32, (CHUNK, width), 0) + (start + row)
                back = jnp.where(place < length, cot[s, pl.ds(row, CHUNK), :].astype(f32), 0.0)
                low = (back * params[taps + 4 : taps + 5, :]).astype(bf16)
                bg[pl.ds(pl.multiple_of(s * quarter + row, CHUNK), CHUNK), :] = low
                wide = low.astype(f32)
                wide = wide[0:8] + wide[8:16]
                total = wide if total is None else total + wide
            bg_sum[...] += total
            return 0

        lax.fori_loop(0, quarter // (GROUP * CHUNK), step, 0)
        tail = own_rows + s * HALO
        put_rows([(tail, [(EDGE, EDGE), (2 * EDGE + quarter, EDGE)])])
        edge = jnp.concatenate([left[s, 1].astype(f32), right[s, 1].astype(f32)], axis=0)
        ids = lax.broadcasted_iota(jnp.int32, (HALO, width), 0)
        place = jnp.where(ids < EDGE, start - EDGE + ids, start + quarter - EDGE + ids)
        back = jnp.where(place < length, edge, 0.0)
        bg[tail : tail + HALO, :] = (back * params[taps + 4 : taps + 5, :]).astype(bf16)
        own = slice(s * quarter, (s + 1) * quarter)
        normed_t[:, own] = normed[own, :].T
        bg_t[:, own] = bg[own, :].T


TILE = 256


def hidden_kernel(slots, taps, dp_count, own_width, own_rows, fast, ints, normed, bg, normed_t, bg_t, params, *refs):
    sources, refs = (refs[:4], refs[4:]) if fast else (refs[:2], refs[2:])
    act, hg, *grads, bias_grad, up, down, hid_a, hid_b, pull_a, pull_b = refs
    all_rows, width = normed.shape
    wide = 2 * own_width
    rows_dp = width // dp_count
    dp_own, core = ints[slots + 1], ints[slots + 2]

    if fast:
        for n in range(2):
            for c in range(2):
                @pl.when(core == c)
                def _():
                    for dp_rel in range(dp_count):
                        rows = pl.ds(pl.multiple_of((dp_rel ^ dp_own) * rows_dp, rows_dp), rows_dp)
                        for x_rel in range(2):
                            place = position(c ^ n, dp_rel, x_rel)
                            source = sources[2 * n + (place >> 3)]
                            columns = slice(n * wide + x_rel * own_width, n * wide + (x_rel + 1) * own_width)
                            up[rows, columns] = source[place & 7, :, 0:own_width]
                            down[rows, columns] = source[place & 7, :, own_width : 2 * own_width]
    else:
        up[...] = sources[0][...]
        down[...] = sources[1][...]

    base = taps + 5
    bias = [
        jnp.concatenate(
            [params[pl.ds(base + ints[slots + 3 + 2 * n + x], 1), 0:own_width] for x in range(2)], axis=1
        )
        for n in range(2)
    ]
    thirds = [slice(k * (own_rows // 3), (k + 1) * (own_rows // 3)) for k in range(3)]
    thirds[2] = slice(thirds[2].start, all_rows)
    stages = [(n, rows) for n in (1, 0) for rows in thirds]

    def products(k):
        n, rows = stages[k]
        count = rows.stop - rows.start
        hid, pull = ((hid_a, pull_a), (hid_b, pull_b))[k % 2]

        def one(out, left, right, column):
            columns = slice(n * wide + column, n * wide + column + TILE)
            out[0:count, column : column + TILE] = jnp.dot(left[rows, :], right[:, columns], preferred_element_type=f32)

        return [
            functools.partial(one, out, left, right, column)
            for column in range(0, wide, TILE)
            for out, left, right in ((hid, normed, up), (pull, bg, down))
        ]

    def elementwise(k):
        n, rows = stages[k]
        count = rows.stop - rows.start
        hid, pull = ((hid_a, pull_a), (hid_b, pull_b))[k % 2]

        def one(sub, column):
            source = (slice(sub, sub + CHUNK), slice(column, column + TILE))
            first = rows.start + sub
            place = (slice(first, first + CHUNK), slice(n * wide + column, n * wide + column + TILE))
            v = hid[source] + bias[n][:, column : column + TILE]
            fall = jnp.exp2(v * v * (-0.5 * 1.4426950408889634))
            t = 1.0 / (1.0 + jnp.abs(v) * (0.3275911 * 0.7071067811865476))
            tail = 0.5 * -1.453152027 + t * (0.5 * 1.061405429)
            tail = 0.5 * 1.421413741 + t * tail
            tail = 0.5 * -0.284496736 + t * tail
            tail = 0.5 * 0.254829592 + t * tail
            tail = t * tail * fall
            below = jnp.where(v < 0.0, tail, 1.0 - tail)
            if first < own_rows:
                act[place] = (v * below).astype(bf16)
            slope = below + v * (fall * 0.3989422804014327)
            hg[place] = (pull[source] * slope).astype(bf16)

        return [
            functools.partial(one, sub, column) for column in range(0, wide, TILE) for sub in range(0, count, CHUNK)
        ]

    def weight_grads(n):
        def one(which, row, column):
            columns = slice(n * wide + column, n * wide + column + TILE)
            left, right = ((normed_t, hg), (bg_t, act))[which]
            value = jnp.dot(left[row : row + TILE, :], right[0:own_rows, columns], preferred_element_type=f32)
            if not fast:
                grads[0][which, row : row + TILE, columns] = value
                return
            value = value.astype(bf16)
            for dp in range(row // rows_dp, (row + TILE) // rows_dp):
                dp_rel = dp ^ dp_own
                high, low, y = (dp_rel >> 2) & 1, (dp_rel >> 1) & 1, dp_rel & 1
                owner = core ^ n
                for x in range(2):
                    first, last = max(column, x * own_width), min(column + TILE, (x + 1) * own_width)
                    if first >= last:
                        continue
                    place = high * (1 + owner) + low * (2 - owner) + 4 * (y * (1 + owner) + x * (2 - owner))
                    out = slice(which * own_width + first - x * own_width, which * own_width + last - x * own_width)
                    grads[n][place, :, out] = value[
                        dp * rows_dp - row : (dp + 1) * rows_dp - row, first - column : last - column
                    ]

        def sums():
            columns = slice(n * wide, (n + 1) * wide)
            bias_grad[:, columns] = jnp.dot(
                jnp.ones((8, own_rows), bf16), hg[0:own_rows, columns], preferred_element_type=f32
            )

        pieces = [
            functools.partial(one, which, row, column)
            for column in range(0, wide, TILE)
            for which in range(2)
            for row in range(0, width, TILE)
        ]
        return pieces + [sums]

    def run(matrix, vector):
        done = 0
        for k, piece in enumerate(matrix):
            piece()
            upto = len(vector) * (k + 1) // len(matrix)
            for other in vector[done:upto]:
                other()
            done = upto

    run(products(0), [])
    run(products(1), elementwise(0))
    run(products(2), elementwise(1))
    run(products(3), elementwise(2))
    grads_1 = weight_grads(1)
    run(products(4) + grads_1[:6], elementwise(3))
    run(products(5) + grads_1[6:], elementwise(4))
    for piece in elementwise(5):
        piece()
    run(weight_grads(0), [])


NT = (((1,), (1,)), ((), ()))


def output_kernel(slots, quarter, width, taps, ints, params, act, down, frames, cot, output, scale_sum, branch):
    s = pl.program_id(0)
    start, length = ints[slots], ints[s]

    @pl.when(s == 0)
    def _():
        scale_sum[...] = jnp.zeros_like(scale_sum)

    own = pl.ds(pl.multiple_of(s * quarter, CHUNK), quarter)
    branch[...] = lax.dot_general(act[own, :], down[...], NT, preferred_element_type=f32)

    def step(i, total_sum):
        row = pl.multiple_of(i * CHUNK, CHUNK)
        rows = pl.ds(row, CHUNK)
        live = lax.broadcasted_iota(jnp.int32, (CHUNK, width), 0) + (start + row) < length
        back = jnp.where(live, cot[s, rows, :].astype(f32), 0.0)
        total = branch[rows, :] + params[taps + 3 : taps + 4, :]
        shown = frames[s, rows, :].astype(f32) + params[taps + 4 : taps + 5, :] * total
        output[0, rows, :] = jnp.where(live, shown, 0.0)
        part = back * total
        return total_sum + (part[0:8] + part[8:16])

    scale_sum[...] += lax.fori_loop(0, quarter // CHUNK, step, jnp.zeros((8, width), f32))


def back_kernel(shape, ints, params, left, right, hg, up, unit, bias_grad, bg_sum, scale_sum,
                frames, cot, input_grad, small, sh, cgs, ngs, ng_halo, acc):
    slots, quarter, width, taps, own_width = shape
    half = taps // 2
    blocks = width // LANES
    own_rows = slots * quarter
    s = pl.program_id(0)
    start = ints[slots]
    length = ints[s]

    def lanes(j):
        return slice(j * LANES, (j + 1) * LANES)

    def product(rows):
        return lax.dot_general(hg[rows, :], up[...], NT, preferred_element_type=f32)

    @pl.when(s == 0)
    def _():
        acc[...] = jnp.zeros_like(acc)
        ng_halo[...] = product(pl.ds(own_rows, slots * HALO))

    fill_shifted(
        s, ints, start, lambda row: frames[s, pl.ds(row, CHUNK), :],
        lambda: left[s, 0], lambda: right[s, 0], sh, quarter, width,
    )
    ngs[...] = product(pl.ds(pl.multiple_of(s * quarter, CHUNK), quarter))

    def norm_back(chunks):
        units, scales, firsts, seconds = [], [], [], []
        for ng, rows in chunks:
            u = [unit[rows, lanes(j)] for j in range(blocks)]
            scaled = [ng[j] * params[taps + 1 : taps + 2, lanes(j)] for j in range(blocks)]
            units.append(u)
            scales.append(scaled)
            firsts.append(functools.reduce(jnp.add, scaled))
            seconds.append(functools.reduce(jnp.add, [a * b for a, b in zip(scaled, u)]))
        firsts = [jnp.sum(v, axis=1, keepdims=True) * (1.0 / width) for v in firsts]
        seconds = [jnp.sum(v, axis=1, keepdims=True) * (1.0 / width) for v in seconds]
        grads = []
        for (_, rows), u, scaled, first, second in zip(chunks, units, scales, firsts, seconds):
            inverse = unit[rows, lanes(blocks)]
            grads.append([inverse * (scaled[j] - first - u[j] * second) for j in range(blocks)])
        return units, grads

    def fold(value):
        return value[0:8] + value[8:16]

    def norm_step(i, _):
        firsts = [pl.multiple_of(i * (GROUP * CHUNK) + u * CHUNK, CHUNK) for u in range(GROUP)]
        ngs_here = [[ngs[pl.ds(row, CHUNK), lanes(j)] for j in range(blocks)] for row in firsts]
        units, grads = norm_back(
            [(ng, pl.ds(pl.multiple_of(s * quarter + row, CHUNK), CHUNK)) for ng, row in zip(ngs_here, firsts)]
        )
        for j in range(blocks):
            for row, cg in zip(firsts, grads):
                cgs[j, pl.ds(row + 2 * EDGE, CHUNK), :] = cg[j]
            acc[taps + 1, :, lanes(j)] += functools.reduce(jnp.add, [fold(ng[j] * u[j]) for ng, u in zip(ngs_here, units)])
            acc[taps + 2, :, lanes(j)] += functools.reduce(jnp.add, [fold(ng[j]) for ng in ngs_here])
            acc[taps, :, lanes(j)] += functools.reduce(jnp.add, [fold(cg[j]) for cg in grads])
        return 0

    lax.fori_loop(0, quarter // (GROUP * CHUNK), norm_step, 0)
    tail = pl.multiple_of(s * HALO, HALO)
    ng = [ng_halo[pl.ds(tail, HALO), lanes(j)] for j in range(blocks)]
    _, (cg,) = norm_back([(ng, pl.ds(pl.multiple_of(own_rows + tail, HALO), HALO))])
    for j in range(blocks):
        cgs[j, 0:EDGE, :] = jnp.zeros((EDGE, LANES), f32)
        cgs[j, EDGE : 2 * EDGE, :] = cg[j][0:EDGE]
        cgs[j, 2 * EDGE + quarter : 3 * EDGE + quarter, :] = cg[j][EDGE:HALO]
        cgs[j, 3 * EDGE + quarter : 4 * EDGE + quarter, :] = jnp.zeros((EDGE, LANES), f32)

    for j in range(blocks):
        def conv_step(i, sums):
            row = pl.multiple_of(i * STRIDE, STRIDE)
            rows = pl.ds(row, STRIDE)
            live = lax.broadcasted_iota(jnp.int32, (STRIDE, LANES), 0) + (start + row) < length
            back = jnp.where(live, cot[s, rows, lanes(j)].astype(f32), 0.0)
            first = row + 2 * EDGE
            here = cgs[j, pl.ds(first, STRIDE), :]
            pulled = jnp.zeros((STRIDE, LANES), f32)
            out = []
            for k in range(taps):
                pulled = pulled + cgs[j, pl.ds(first + half - k, STRIDE), :] * params[k : k + 1, lanes(j)]
                product = here * sh[j, pl.ds(first + k - half, STRIDE), :]
                out.append(sums[k] + functools.reduce(jnp.add, [product[r : r + 8] for r in range(0, STRIDE, 8)]))
            input_grad[0, rows, lanes(j)] = back + jnp.where(live, pulled, 0.0)
            return tuple(out)

        sums = lax.fori_loop(
            0, quarter // STRIDE, conv_step, tuple(jnp.zeros((8, LANES), f32) for _ in range(taps))
        )
        for k in range(taps):
            acc[k, :, lanes(j)] += sums[k]

    @pl.when(s == slots - 1)
    def _():
        small[...] = jnp.zeros_like(small)
        for k in range(taps + 3):
            small[k : k + 1, :] = jnp.sum(acc[k], axis=0, keepdims=True)
        small[taps + 3 : taps + 4, :] = jnp.sum(bg_sum[...], axis=0, keepdims=True)
        small[taps + 4 : taps + 5, :] = jnp.sum(scale_sum[...], axis=0, keepdims=True)
        for x in range(4):
            place = ints[slots + 3 + x]
            small[pl.ds(taps + 5 + place, 1), 0:own_width] = bias_grad[0:1, x * own_width : (x + 1) * own_width]


def update_kernel(keep, arrived, *refs):
    width = refs[0].shape[1]
    for n in range(2):
        weights, moment, square = refs[n], refs[2 + n], refs[4 + n]
        shown = refs[6 + 4 * n : 10 + 4 * n]
        lanes = slice(n * width, (n + 1) * width)
        gradient = keep[0, :, lanes].astype(f32) + arrived[0, :, lanes].astype(f32)
        next_weights, next_moment, next_square, _ = adam_step(
            weights[...], gradient, moment[...], square[...], None
        )
        shown[0][...] = gradient
        shown[1][...] = next_weights
        shown[2][...] = next_moment
        shown[3][...] = next_square


def finish_kernel(taps, ints, small, *refs):
    own_channels, own_bias = refs[0].shape[1], refs[6].shape[1]
    own = ints[0]
    shift = own * own_channels
    width = small.shape[1]
    channels = pltpu.roll(small[0:16, :], width - shift, 1)
    bias_row = small[pl.ds(ints[1], 1), :]
    bias = pltpu.roll(jnp.broadcast_to(bias_row, (8, width)), width - ints[2], 1)[0:1, 0:own_bias]
    for n in range(7):
        rows = slice(0, taps) if n == 0 else slice(taps + n - 1, taps + n)
        gradient = bias if n == 6 else channels[rows, 0:own_channels]
        shown = refs[21 + 4 * n : 25 + 4 * n]
        next_weights, next_moment, next_square, update = adam_step(
            refs[n][...], gradient, refs[7 + n][...], refs[14 + n][...], None
        )
        shown[0][...] = gradient
        shown[1][...] = update if n in (2, 5) else next_weights
        shown[2][...] = next_moment
        shown[3][...] = next_square


def call(kernel, outs, in_specs, scratch, limit, flops=0, moved=0, grid=None, out_specs=None):
    grid_spec = pltpu.PrefetchScalarGridSpec(
        num_scalar_prefetch=0,
        grid=grid or (),
        in_specs=in_specs,
        out_specs=out_specs or [vmem()] * len(outs),
        scratch_shapes=scratch,
    )
    return pl.pallas_call(
        kernel,
        out_shape=[jax.ShapeDtypeStruct(shape, dtype) for shape, dtype in outs],
        grid_spec=grid_spec,
        compiler_params=pltpu.CompilerParams(vmem_limit_bytes=limit * MIB),
        cost_estimate=pl.CostEstimate(flops=flops, bytes_accessed=moved, transcendentals=0),
    )


def per_device(
    dp_count,
    tp_count,
    frames,
    cotangent,
    lengths,
    conv_weight,
    conv_bias,
    norm_gain,
    norm_bias,
    up_weight,
    up_bias,
    down_weight,
    down_bias,
    layer_scale,
    moment_conv_weight,
    moment_conv_bias,
    moment_norm_gain,
    moment_norm_bias,
    moment_up_weight,
    moment_up_bias,
    moment_down_weight,
    moment_down_bias,
    moment_layer_scale,
    square_conv_weight,
    square_conv_bias,
    square_norm_gain,
    square_norm_bias,
    square_up_weight,
    square_up_bias,
    square_down_weight,
    square_down_bias,
    square_layer_scale,
):
    both = ("dp", "tp")
    count = dp_count * tp_count
    dp_own, tp_own = lax.axis_index("dp"), lax.axis_index("tp")
    own = dp_own * tp_count + tp_own
    slots, quarter, width = frames.shape
    own_channels, taps = conv_weight.shape
    own_bias = up_bias.shape[0]
    own_rows_w, own_width = up_weight.shape
    hidden_width = own_width * tp_count
    all_rows = slots * (quarter + HALO)
    own_rows = slots * quarter
    fast = (dp_count, tp_count) == (8, 4) and own_rows_w % CHUNK == 0
    core = own & 1

    def swap(value, masks):
        return lax.ppermute(value, both, [(i, i ^ masks[i & 1]) for i in range(count)])

    if fast:
        steps = [(FAST_MASKS[0][k], FAST_MASKS[1][k]) for k in range(4)]
        none = jnp.zeros((), bf16)
        held = (
            lax.pad(up_weight.astype(bf16), none, ((0, 0, 0), (0, own_width, 0)))
            + lax.pad(down_weight.astype(bf16), none, ((0, 0, 0), (own_width, 0, 0)))
        )[None]
        for k in range(3):
            arrived = swap(held, steps[k])
            held = jnp.concatenate([held, arrived], axis=0)
        far = swap(held, steps[3])
        other = swap(held, (1, 1))
        other_far = swap(far, (1, 1))
        weights = (held, far, other, other_far)
        blocks = [[tp_own ^ (2 * x + n) for x in range(2)] for n in range(2)]
    else:
        weights = [
            lax.all_gather(lax.all_gather(w.astype(bf16), "dp", axis=0, tiled=True), "tp", axis=1, tiled=True)
            for w in (up_weight, down_weight)
        ]
        blocks = [[jnp.int32(2 * n + x) for x in range(2)] for n in range(2)]

    pair = jnp.stack([frames, cotangent], axis=1)
    left = lax.ppermute(pair[:, :, quarter - EDGE :, :], "tp", [(i, i + 1) for i in range(tp_count - 1)])
    right = lax.ppermute(pair[:, :, :EDGE, :], "tp", [(i + 1, i) for i in range(tp_count - 1)])

    small_rows = taps + 5 + tp_count
    channels = jnp.concatenate(
        [conv_weight.T, conv_bias[None], norm_gain[None], norm_bias[None], down_bias[None], layer_scale[None]], axis=0
    )
    params = jnp.zeros((small_rows, width), f32)
    params = lax.dynamic_update_slice(params, channels, (0, own * own_channels))
    params = lax.dynamic_update_slice(
        params, up_bias[None], (taps + 5 + own * own_bias // own_width, own * own_bias % own_width)
    )
    bits = [(1 << k, 1 << k) for k in range(count.bit_length() - 1)]
    assert 1 << len(bits) == count

    def sum_all(value, order):
        for masks in order:
            arrived = swap(value, masks)
            value = value + arrived
        return value

    params = sum_all(params, FEW_ORDER if fast else bits)

    ints = jnp.stack(
        [*[lengths[s] for s in range(slots)], tp_own * quarter, dp_own, core, *blocks[0], *blocks[1]]
    ).astype(jnp.int32)

    front = call(
        functools.partial(front_kernel, slots, quarter, width, taps),
        [
            ((all_rows, width), bf16),
            ((all_rows, width + LANES), f32),
            ((all_rows, width), bf16),
            ((width, own_rows), bf16),
            ((width, own_rows), bf16),
            ((8, width), f32),
        ],
        [smem(), vmem(), vmem(), vmem(), vmem(), vmem()],
        [pltpu.VMEM((width // LANES, quarter + 4 * EDGE, LANES), f32)],
        4, flops=10 * all_rows * width * taps, moved=8 * all_rows * width,
    )
    normed, unit, bg, normed_t, bg_t, bg_sum = front(ints, frames, cotangent, left, right, params)

    wide = 2 * own_width
    grads_shape = (2 * dp_count, own_rows_w, wide)
    most = own_rows // 3 + all_rows - own_rows
    hidden = call(
        functools.partial(hidden_kernel, slots, taps, dp_count, own_width, own_rows, fast),
        [((own_rows, hidden_width), bf16), ((all_rows, hidden_width), bf16)]
        + ([(grads_shape, bf16)] * 2 if fast else [((2, width, hidden_width), f32)])
        + [((8, hidden_width), f32), ((width, hidden_width), bf16), ((width, hidden_width), bf16)],
        [smem()] + [vmem()] * (5 + len(weights)),
        [pltpu.VMEM((most, wide), f32)] * 4,
        10, flops=8 * all_rows * width * hidden_width, moved=8 * all_rows * hidden_width,
    )
    act, hg, *grads, bias_grad, up, down = hidden(ints, normed, bg, normed_t, bg_t, params, *weights)

    slot_spec = pl.BlockSpec((1, quarter, width), lambda s: (s, 0, 0))
    output = call(
        functools.partial(output_kernel, slots, quarter, width, taps),
        [((slots, quarter, width), f32), ((8, width), f32)],
        [smem()] + [vmem()] * 5,
        [pltpu.VMEM((quarter, width), f32)],
        8, flops=2 * own_rows * width * hidden_width, moved=8 * all_rows * width,
        grid=(slots,), out_specs=[slot_spec, vmem()],
    )
    output_own, scale_sum = output(ints, params, act, down, frames, cotangent)
    back = call(
        functools.partial(back_kernel, (slots, quarter, width, taps, own_width)),
        [((slots, quarter, width), f32), ((small_rows, width), f32)],
        [smem()] + [vmem()] * 11,
        [
            pltpu.VMEM((width // LANES, quarter + 4 * EDGE, LANES), f32),
            pltpu.VMEM((width // LANES, quarter + 4 * EDGE, LANES), f32),
            pltpu.VMEM((quarter, width), f32),
            pltpu.VMEM((slots * HALO, width), f32),
            pltpu.VMEM((taps + 5, 8, width), f32),
        ],
        8, flops=2 * all_rows * width * hidden_width, moved=8 * all_rows * width,
        grid=(slots,), out_specs=[slot_spec, vmem()],
    )
    input_own, small = back(ints, params, left, right, hg, up, unit, bias_grad, bg_sum, scale_sum, frames, cotangent)

    if fast:
        def plus(a, b):
            return (a.astype(f32) + b.astype(f32)).astype(bf16)

        arrived = swap(grads[1], (1, 1))
        keep, send = plus(grads[0][:8], arrived[:8]), plus(grads[0][8:], arrived[8:])
        for k in range(3, 0, -1):
            size = keep.shape[0] // 2
            arrived = swap(send, steps[k])
            send = plus(keep[size:], arrived[size:])
            keep = plus(keep[:size], arrived[:size])
        arrived = swap(send, steps[0])
        shape = (own_rows_w, own_width)
        updated = call(
            update_kernel, [(shape, f32)] * 8, [vmem()] * 8, [], 4,
            flops=40 * own_rows_w * own_width, moved=64 * own_rows_w * own_width,
            out_specs=[whole(shape)] * 8,
        )(
            keep, arrived, up_weight, down_weight, moment_up_weight, moment_down_weight,
            square_up_weight, square_down_weight,
        )
        updated = {4: tuple(updated[:4]), 6: tuple(updated[4:])}
        up_share = down_share = None
    else:
        updated = {}
        up_share, down_share = (
            lax.psum_scatter(
                lax.psum_scatter(grads[0][n], "tp", scatter_dimension=1, tiled=True),
                "dp", scatter_dimension=0, tiled=True,
            )
            for n in range(2)
        )

    small = sum_all(small, SUM_ORDER if fast else bits)
    order = (0, 1, 2, 3, 7, 8, 5)
    lists = (
        (conv_weight, conv_bias, norm_gain, norm_bias, up_weight, up_bias, down_weight, down_bias, layer_scale),
        (
            moment_conv_weight, moment_conv_bias, moment_norm_gain, moment_norm_bias, moment_up_weight,
            moment_up_bias, moment_down_weight, moment_down_bias, moment_layer_scale,
        ),
        (
            square_conv_weight, square_conv_bias, square_norm_gain, square_norm_bias, square_up_weight,
            square_up_bias, square_down_weight, square_down_bias, square_layer_scale,
        ),
    )
    given = [v.T if v.ndim == 2 else v[None] for values in lists for v in [values[n] for n in order]]
    shapes = [v.shape for v in given[:7]]
    finished = call(
        functools.partial(finish_kernel, taps),
        [(shape, f32) for shape in shapes for _ in range(4)],
        [smem(), vmem()] + [vmem()] * 21, [], 4,
        out_specs=[whole(shape) for shape in shapes for _ in range(4)],
    )(
        jnp.stack([own, taps + 5 + own * own_bias // own_width, own * own_bias % own_width]).astype(jnp.int32),
        small, *given,
    )
    for k, n in enumerate(order):
        values = finished[4 * k : 4 * k + 4]
        updated[n] = tuple(v.T if n == 0 else v[0] for v in values)
    step_number = jnp.float32(STEP)
    params_own = (
        conv_weight,
        conv_bias,
        norm_gain,
        norm_bias,
        up_weight,
        up_bias,
        down_weight,
        down_bias,
        layer_scale,
    )
    gradients = (None,) * 4 + (up_share, None, down_share, None, None)
    moments = (
        moment_conv_weight,
        moment_conv_bias,
        moment_norm_gain,
        moment_norm_bias,
        moment_up_weight,
        moment_up_bias,
        moment_down_weight,
        moment_down_bias,
        moment_layer_scale,
    )
    squares = (
        square_conv_weight,
        square_conv_bias,
        square_norm_gain,
        square_norm_bias,
        square_up_weight,
        square_up_bias,
        square_down_weight,
        square_down_bias,
        square_layer_scale,
    )
    flat = [output_own, input_own]
    for n, (weights_now, gradient, moment, square, use_update) in enumerate(
        zip(params_own, gradients, moments, squares, update_flags)
    ):
        if n in updated:
            flat = flat + [*updated[n]]
            continue
        next_weights, next_moment, next_square, update = adam_step(weights_now, gradient, moment, square, step_number)
        shown = update if use_update else next_weights
        flat = flat + [gradient, shown, next_moment, next_square]
    return tuple(flat)


def body(dp_count, tp_count, *args):
    return per_device(dp_count, tp_count, *args)


def solution(mesh):
    vector, matrix = P(("dp", "tp")), P("dp", "tp")
    taps = P(("dp", "tp"), None)
    frames = P("dp", "tp", None)
    parameters = (taps, vector, vector, vector, matrix, vector, matrix, vector, vector)
    return jax.shard_map(
        functools.partial(body, mesh.shape["dp"], mesh.shape["tp"]),
        mesh=mesh,
        in_specs=(frames, frames, P("dp")) + parameters * 3,
        out_specs=(frames, frames) + tuple(spec for spec in parameters for _ in range(4)),
        check_vma=False,
    )
```
